128 devices in a mesh: tp: 2 (over core), ep: 64 (over z, y, x).
Axes of the slice: x: 4, y: 4, z: 4, core: 2. Of those that a mesh axis runs over, the one named last changes fastest.
Arguments:
- context: bfloat16 [64, 256, 2048], P('ep', None, 'tp'), may hold values from -6 to 6
- out_weight: bfloat16 [2048, 2048], P('tp'), may hold values from -0.125 to 0.125
- residual_in: bfloat16 [64, 256, 2048], P('ep', 'tp'), may hold values from -6 to 6
- norm_gain: float32 [2048], replicated, may hold values from 0.5 to 1.5
- expert_ids: int32 [64, 256, 2], P('ep', 'tp'), may hold values from 0 to 63, all different within a row; in each aligned block of 128 rows (0 to 127, 128 to 255, ..., all dimensions but the last counted through in order) at most 6 rows name the same one
- gate_weights: float32 [64, 256, 2], P('ep', 'tp'), may hold values from 0.2 to 1
- keep_mask: int32 [64, 256, 2], P('ep', 'tp'), may hold values 0 or 1
- expert_in: bfloat16 [64, 2048, 4096], P('ep', None, 'tp'), may hold values from -0.125 to 0.125
- expert_out: bfloat16 [64, 4096, 2048], P('ep', 'tp'), may hold values from -0.09375 to 0.09375
Outputs:
- layer_out: bfloat16 [64, 256, 2048], P('ep', 'tp')
The draws below stay inside these ranges and needn't reach their ends.
Inputs may be any that keep to these rules, and one draw needn't show every extreme that they name: `expert_ids`: among the 128 tokens of one device (aligned blocks of token rows), at most 6 name any one expert; a token's two experts differ; every expert is named somewhere.
All inputs are finite; a program needn't handle non-finite values. No bound on the sum of `keep_mask` on one device may be relied on, other than what follows from the above.
Results may differ from the reference program's by a relative error of at most 0.0054.
Values may be sent and summed in bfloat16 or wider, within the bound.
No kernel may reach another device: no remote copies, remote signals or barrier semaphores. Data moves between devices by JAX's collectives and lax.ppermute only.
A program may use at most 128 MiB of HBM per device.

```python
import math
import jax
import jax.numpy as jnp
import numpy as np
from jax import lax

D = 2048
FF = 4096
TOK_DEV = 128
TOK_EP = 256
EXPERTS = 64
SLOT = 6
N_EP = 64


def set_ends(result, own_key, low, top_value):
    index_at = [jax.random.randint(jax.random.fold_in(own_key, axis), (), 0, length) for axis, length in enumerate(result.shape)]
    main_axis = result.shape.index(max(result.shape))
    next_to = index_at[:main_axis] + [(index_at[main_axis] + 1) % result.shape[main_axis]] + index_at[main_axis + 1:]
    return result.at[tuple(index_at)].set(low).at[tuple(next_to)].set(top_value)


def level_of(key, dims, pieces, low, high):
    def one(position, shards_of):
        draws = jax.random.uniform(jax.random.fold_in(jax.random.fold_in(key, 6), position), (shards_of,), jnp.float32, low / len(pieces), high / len(pieces))
        return jnp.repeat(jnp.exp(draws), dims[position] // shards_of).reshape((-1,) + (1,) * (len(dims) - position - 1))

    factor_of = one(*pieces[0])
    for cut in pieces[1:]:
        factor_of = factor_of * one(*cut)
    return factor_of


def deal_out(own_key, own, number, rows, amount, top, reach, slope):
    ranking = jax.random.permutation(own_key, amount)
    crowded, usual = portions_of(amount, rows * top, reach, slope, True), portions_of(amount, rows * top, reach, slope, False)
    places = jnp.arange(amount)

    def named(sizes, offset_by):
        used = int((sizes > 0).sum())
        fixed = max(1, used // 4)
        passed = fixed + (places - fixed + offset_by * (used - fixed)) % max(1, amount - fixed)
        return jnp.zeros((amount,), jnp.int32).at[ranking[jnp.where(places < fixed, places, passed)]].set(jnp.asarray(sizes, jnp.int32))

    sizes = jnp.where(number % 4 == 0, named(crowded, number // 4), named(usual, number - number // 4 - 1))
    mixed = jax.random.permutation(jax.random.fold_in(own, 3), amount)
    donor, receiver = mixed[0:amount // 2 * 2:2], mixed[1:amount // 2 * 2:2]
    margin = jnp.minimum(sizes[donor] - 1, reach - sizes[receiver]) // 2
    margin = jnp.where((donor == ranking[0]) | (receiver == ranking[0]) | (sizes[receiver] == 0), 0, jnp.maximum(margin, 0))
    passed = jax.random.randint(jax.random.fold_in(own, 4), (amount // 2,), 0, 1 << 20) % (margin + 1)
    sizes = sizes.at[donor].add(-passed).at[receiver].add(passed)
    members = jnp.searchsorted(jnp.cumsum(sizes), jnp.arange(rows * top), side="right").astype(jnp.int32)
    listing = members.reshape(top, rows).T
    listing = listing[jax.random.permutation(jax.random.fold_in(own, 1), rows)]
    offset_by = jax.random.randint(jax.random.fold_in(own, 2), (rows, 1), 0, top)
    return jnp.take_along_axis(listing, (jnp.arange(top)[None, :] + offset_by) % top, axis=1)


def portions_of(amount, total, most, skew, full):
    loads = [(1 << 20) // math.isqrt(standing ** skew) + 1 for standing in range(1, amount + 1)]
    largest = most if full else min(most, max(-(-total // amount), total * loads[0] // sum(loads)))
    least = 1 if total - largest >= amount - 1 else 0
    holding, surplus = [largest] + [least] * (amount - 1), total - largest - least * (amount - 1)
    while surplus > 0:
        free = [i for i in range(1, amount) if holding[i] < largest] or [i for i in range(1, amount) if holding[i] < most]
        pool, remaining = sum([loads[i] for i in free]), surplus
        for i in free:
            more = min(most - holding[i], max(1, remaining * loads[i] // pool), surplus)
            holding[i] = holding[i] + more
            surplus = surplus - more
    return np.array(holding)


def noise(rng, dims, width, limit, pieces=(), kind=jnp.bfloat16):
    array = jax.random.normal(rng, dims, jnp.float32) * width
    if len(pieces) > 0:
        array = level_of(rng, dims, pieces, -0.22, 0.18) * array
    return jnp.clip(array, min=-limit, max=limit).astype(kind)


def setup_inputs(seed: int = 0) -> dict:
    seeds = jax.random.split(jax.random.key(seed), 10)
    context = noise(seeds[0], (N_EP, TOK_EP, D), 1.0, 6.0, ((0, 64), (2, 2)))
    out_weight = noise(seeds[1], (D, D), D ** -0.5, 0.125, ((0, 2),))
    residual_in = noise(seeds[2], (N_EP, TOK_EP, D), 1.0, 6.0, ((0, 64), (1, 2)))
    norm_gain = jnp.clip(1.0 + 0.1 * jax.random.normal(seeds[3], (D,), jnp.float32), 0.5, 1.5)
    expert_ids_keys = jax.random.split(jax.random.fold_in(seeds[4], 1), N_EP * TOK_EP // TOK_DEV)
    expert_ids_turns = jax.random.permutation(jax.random.fold_in(seeds[4], 3), N_EP * TOK_EP // TOK_DEV)
    expert_ids = jax.vmap(lambda own, number: deal_out(jax.random.fold_in(seeds[4], 2), own, number, TOK_DEV, EXPERTS, 2, SLOT, 2))(expert_ids_keys, expert_ids_turns).reshape((N_EP, TOK_EP, 2))
    gate_weights = jnp.clip(0.2 + 0.8 * jax.random.uniform(seeds[5], (N_EP, TOK_EP, 2), jnp.float32) ** level_of(seeds[5], (N_EP, TOK_EP, 2), ((0, 64), (1, 2)), -0.2, 0.2), 0.2, 1.0)
    keep_mask = set_ends((jax.random.randint(seeds[6], (N_EP, TOK_EP, 2), 0, 8) < 7).astype(jnp.int32), jax.random.fold_in(seeds[6], 1), 0, 1)
    expert_in = noise(seeds[7], (EXPERTS, D, FF), D ** -0.5, 0.125, ((0, 64), (2, 2)))
    expert_out = noise(seeds[8], (EXPERTS, FF, D), FF ** -0.5, 0.09375, ((0, 64), (1, 2)))
    return dict(context=context, out_weight=out_weight, residual_in=residual_in, norm_gain=norm_gain, expert_ids=expert_ids, gate_weights=gate_weights, keep_mask=keep_mask, expert_in=expert_in, expert_out=expert_out)


def reference(context, out_weight, residual_in, norm_gain, expert_ids, gate_weights, keep_mask, expert_in, expert_out):
    flat_context = context.reshape(-1, D)
    attended = jnp.dot(flat_context, out_weight, preferred_element_type=jnp.float32)
    stream = (residual_in.reshape(-1, D).astype(jnp.float32) + attended).astype(jnp.bfloat16)
    stream_f32 = stream.astype(jnp.float32)
    average = lax.optimization_barrier(jnp.mean(stream_f32, axis=1, keepdims=True))
    centred = stream_f32 - average
    variance = lax.optimization_barrier(jnp.mean(centred * centred, axis=1, keepdims=True))
    normed = (centred / jnp.sqrt(variance + 1e-05) * norm_gain[None, :]).astype(jnp.bfloat16)
    routed = expert_ids.reshape(-1)
    kept_flags = keep_mask.reshape(-1)
    assign_count = routed.shape[0]
    row_bound = 2 * N_EP * SLOT

    def one_expert(collected, inputs):
        expert_index, weight_in, weight_out = inputs
        chosen = (routed == expert_index) & (kept_flags > 0)
        positions = jnp.nonzero(chosen, size=row_bound, fill_value=assign_count)[0].astype(jnp.int32)
        picked_rows = normed[jnp.minimum(positions, assign_count - 1) // 2]
        hidden = jnp.maximum(jnp.dot(picked_rows, weight_in, preferred_element_type=jnp.float32), 0.0).astype(jnp.bfloat16)
        expert_rows = jnp.dot(hidden, weight_out, preferred_element_type=jnp.float32).astype(jnp.bfloat16)
        return (collected.at[positions].set(expert_rows, mode='drop'), None)
    collected, _ = lax.scan(one_expert, jnp.zeros((assign_count, D), jnp.bfloat16), (jnp.arange(EXPERTS, dtype=jnp.int32), expert_in, expert_out))
    gate_flat = jnp.where(kept_flags > 0, gate_weights.reshape(-1), 0.0).astype(jnp.float32)
    mixed = gate_flat[:, None] * collected.astype(jnp.float32)
    mixed = lax.optimization_barrier(jnp.sum(mixed.reshape(-1, 2, D), axis=1))
    layer_out = (stream_f32 + mixed).astype(jnp.bfloat16)
    return layer_out.reshape(N_EP, TOK_EP, D)
```

```python
import functools

import jax
import jax.numpy as jnp
from jax import lax
from jax.experimental import pallas as pl
from jax.experimental.pallas import tpu as pltpu
from jax.sharding import PartitionSpec as P

SLOT = 6
PACK = 8
F32, BF16 = jnp.float32, jnp.bfloat16
VMEM = pl.BlockSpec(memory_space=pltpu.VMEM)


def dot(a, b):
    return jnp.dot(a, b, preferred_element_type=F32)


def iota(shape, dim):
    return lax.broadcasted_iota(jnp.int32, shape, dim)


def places(ids, keep, experts, along):
    tokens = ids[0].shape[along]
    shape = (experts, tokens) if along == 1 else (tokens, experts)
    member = iota(shape, 1 - along)
    hot = [jnp.where((member == ids[k]) & (keep[k] > 0), 1.0, 0.0) for k in (0, 1)]
    older = (iota((tokens, tokens), 1 - along) < iota((tokens, tokens), along)).astype(F32).astype(BF16)
    out = []
    base = 0.0
    for k in (0, 1):
        sent = hot[k].astype(BF16)
        before = (dot(sent, older) if along == 1 else dot(older, sent)) + base
        rank = jnp.sum(hot[k] * before, axis=1 - along, keepdims=True).astype(jnp.int32)
        base = base + jnp.sum(hot[k], axis=along, keepdims=True)
        late = jnp.where(rank >= SLOT // 2, 1, 0)
        block = rank - (SLOT // 2) * late
        kept = keep[k] > 0
        main = jnp.where(kept, ids[k] * PACK + rank, -1)
        tail = ids[k] * PACK + SLOT + late
        out.append((main, [jnp.where(kept & (block == j), tail, -1) for j in range(3)]))
    return out


def pack_kernel(experts, own_ref, recv_ref, res_ref, gain_ref, ids_ref, keep_ref, stream_ref, packed_ref):
    stream = (res_ref[...].astype(F32) + (own_ref[...] + recv_ref[...])).astype(BF16)
    stream_ref[...] = stream
    value = stream.astype(F32)
    count = value.shape[1]
    centred = value - jnp.sum(value, axis=1, keepdims=True) / count
    variance = jnp.sum(centred * centred, axis=1, keepdims=True) / count
    normed = (centred / jnp.sqrt(variance + 1e-05) * gain_ref[...]).astype(BF16)
    ids = [ids_ref[k : k + 1, :] for k in (0, 1)]
    keep = [keep_ref[k : k + 1, :] for k in (0, 1)]
    (main0, tails0), (main1, tails1) = places(ids, keep, experts, 1)
    rows = iota((experts * PACK, ids[0].shape[1]), 0)

    def choose(a, b):
        return jnp.where((rows == a) | (rows == b), 1.0, 0.0).astype(BF16)

    main = choose(main0, main1)
    wide = count * SLOT // PACK
    part = wide // 3
    for j in range(3):
        packed_ref[:, j * part : (j + 1) * part] = (
            dot(main, normed[:, j * part : (j + 1) * part])
            + dot(choose(tails0[j], tails1[j]), normed[:, wide:])
        ).astype(BF16)


def combine_kernel(experts, packed_ref, stream_ref, ids_ref, keep_ref, gate_ref, out_ref):
    ids = [ids_ref[:, k : k + 1] for k in (0, 1)]
    keep = [keep_ref[:, k : k + 1] for k in (0, 1)]
    (main0, tails0), (main1, tails1) = places(ids, keep, experts, 0)
    tokens = ids[0].shape[0]
    columns = iota((tokens, experts * PACK), 1)

    def choose(a):
        return jnp.where(columns == a, 1.0, 0.0).astype(BF16)

    gates = [gate_ref[:, k : k + 1] for k in (0, 1)]
    wide = packed_ref.shape[1]
    part = wide // 3
    mains = [choose(main0), choose(main1)]
    tails = [[choose(tails0[j]), choose(tails1[j])] for j in range(3)]
    for j in range(3):
        block = packed_ref[:, j * part : (j + 1) * part]
        mixed = gates[0] * dot(mains[0], block) + gates[1] * dot(mains[1], block)
        at = slice(j * part, (j + 1) * part)
        out_ref[:, at] = (stream_ref[:, at].astype(F32) + mixed).astype(BF16)
    mixed = 0.0
    for k in (0, 1):
        mixed += gates[k] * sum(dot(tails[j][k], packed_ref[:, j * part : (j + 1) * part]) for j in range(3))
    out_ref[:, wide:] = (stream_ref[:, wide:].astype(F32) + mixed).astype(BF16)


SOURCES = 32


def unpack_into(packed_ref, rows_ref):
    tall, short = SOURCES * PACK, SOURCES * SLOT
    wide = packed_ref.shape[1]
    part = wide // 3
    row, col = iota((short, tall), 0), iota((short, tall), 1)
    source, at = col >> 3, col & 7
    first = row - SLOT * source
    main = jnp.where((at < SLOT) & (first == at), 1.0, 0.0).astype(BF16)
    tails = [
        jnp.where((at >= SLOT) & (first == (at - SLOT) * 3 + j), 1.0, 0.0).astype(BF16)
        for j in range(3)
    ]
    for g in range(packed_ref.shape[0] // tall):
        block = packed_ref[g * tall : (g + 1) * tall, :]
        at_rows = slice(g * short, (g + 1) * short)
        rows_ref[at_rows, :wide] = dot(main, block).astype(BF16)
        rows_ref[at_rows, wide:] = sum(
            dot(tails[j], block[:, j * part : (j + 1) * part]) for j in range(3)
        ).astype(BF16)


def ffn_kernel(packed_ref, in_ref, out_ref, result_ref, rows_ref, acc_ref):
    step = pl.program_id(0)

    @pl.when(step == 0)
    def _():
        unpack_into(packed_ref, rows_ref)

    hidden = jnp.maximum(dot(rows_ref[...], in_ref[...]), 0.0).astype(BF16)
    term = dot(hidden, out_ref[...])

    @pl.when(step == 0)
    def _():
        acc_ref[...] = term

    @pl.when(step > 0)
    def _():
        acc_ref[...] += term

    @pl.when(step == pl.num_programs(0) - 1)
    def _():
        result_ref[...] = acc_ref[...].astype(result_ref.dtype)


def ffn(packed, weight_in, weight_out, dtype, tile=512):
    rows = packed.shape[0] * SLOT // PACK
    features, units = weight_in.shape
    return pl.pallas_call(
        ffn_kernel,
        grid=(units // tile,),
        in_specs=[
            pl.BlockSpec(packed.shape, lambda f: (0, 0), pipeline_mode=pl.Buffered(1)),
            pl.BlockSpec((features, tile), lambda f: (0, f)),
            pl.BlockSpec((tile, features), lambda f: (f, 0)),
        ],
        out_specs=pl.BlockSpec((rows, features), lambda f: (0, 0)),
        out_shape=jax.ShapeDtypeStruct((rows, features), dtype),
        scratch_shapes=[pltpu.VMEM((rows, features), BF16), pltpu.VMEM((rows, features), F32)],
        compiler_params=pltpu.CompilerParams(vmem_limit_bytes=48 << 20),
        cost_estimate=pl.CostEstimate(
            flops=4 * rows * features * units, bytes_accessed=4 * features * units, transcendentals=0
        ),
        name="ffn",
    )(packed, weight_in, weight_out)


def repack_kernel(own_ref, recv_ref, packed_ref):
    tall, short = SOURCES * PACK, SOURCES * SLOT
    wide = packed_ref.shape[1]
    part = wide // 3
    row, col = iota((tall, short), 1), iota((tall, short), 0)
    source, at = col >> 3, col & 7
    first = row - SLOT * source
    main = jnp.where((at < SLOT) & (first == at), 1.0, 0.0).astype(BF16)
    tails = [
        jnp.where((at >= SLOT) & (first == (at - SLOT) * 3 + j), 1.0, 0.0).astype(BF16)
        for j in range(3)
    ]
    for g in range(packed_ref.shape[0] // tall):
        at_rows = slice(g * short, (g + 1) * short)
        block = (own_ref[at_rows, :] + recv_ref[at_rows, :].astype(F32)).astype(BF16)
        for j in range(3):
            packed_ref[g * tall : (g + 1) * tall, j * part : (j + 1) * part] = (
                dot(main, block[:, j * part : (j + 1) * part]) + dot(tails[j], block[:, wide:])
            ).astype(BF16)


def whole(kernel, out_shape, name, flops, *args):
    return pl.pallas_call(
        kernel,
        in_specs=[VMEM] * len(args),
        out_specs=jax.tree.map(lambda _: VMEM, out_shape),
        out_shape=out_shape,
        compiler_params=pltpu.CompilerParams(vmem_limit_bytes=48 << 20),
        cost_estimate=pl.CostEstimate(
            flops=flops, bytes_accessed=sum(a.size * a.dtype.itemsize for a in args), transcendentals=0
        ),
        name=name,
    )(*args)


SWAP = [(0, 1), (1, 0)]


def body(context, out_weight, residual_in, norm_gain, expert_ids, gate_weights, keep_mask, expert_in, expert_out):
    tokens, features = residual_in.shape[1:]
    experts = lax.axis_size("ep")
    core = lax.axis_index("tp")
    other_half = dot(lax.dynamic_slice_in_dim(context[0], (1 - core) * tokens, tokens), out_weight)
    recv = lax.ppermute(other_half, "tp", SWAP)
    own = dot(lax.dynamic_slice_in_dim(context[0], core * tokens, tokens), out_weight)
    wide = features * SLOT // PACK
    packed_shape = jax.ShapeDtypeStruct((experts * PACK, wide), BF16)
    stream, outgoing = whole(
        functools.partial(pack_kernel, experts),
        (jax.ShapeDtypeStruct((tokens, features), BF16), packed_shape),
        "pack",
        4 * tokens * experts * PACK * wide,
        own, recv, residual_in[0], norm_gain[None, :], expert_ids[0].T, keep_mask[0].T,
    )

    def exchange(packed):
        blocks = packed.reshape(experts, PACK, wide)
        return lax.all_to_all(blocks, "ep", split_axis=0, concat_axis=0, tiled=True).reshape(packed.shape)

    rows = exchange(outgoing)
    rows_other = lax.ppermute(rows, "tp", SWAP)
    part_own = ffn(rows, expert_in[0], expert_out[0], F32)
    part_other = ffn(rows_other, expert_in[0], expert_out[0], BF16)
    part_recv = lax.ppermute(part_other, "tp", SWAP)
    results = whole(
        repack_kernel, packed_shape, "repack", 4 * SOURCES * SLOT * experts * PACK * wide, part_own, part_recv
    )
    returned = exchange(results)
    return whole(
        functools.partial(combine_kernel, experts),
        jax.ShapeDtypeStruct((tokens, features), BF16),
        "combine",
        8 * tokens * experts * PACK * wide,
        returned, stream, expert_ids[0], keep_mask[0], gate_weights[0],
    )[None]


def solution(mesh):
    return jax.shard_map(
        body,
        mesh=mesh,
        in_specs=(
            P("ep", None, "tp"),
            P("tp", None),
            P("ep", "tp", None),
            P(),
            P("ep", "tp", None),
            P("ep", "tp", None),
            P("ep", "tp", None),
            P("ep", None, "tp"),
            P("ep", "tp", None),
        ),
        out_specs=P("ep", "tp", None),
        check_vma=False,
    )
```

```python
import functools

import jax
import jax.numpy as jnp
from jax import lax
from jax.experimental import pallas as pl
from jax.experimental.pallas import tpu as pltpu
from jax.sharding import PartitionSpec as P


PACK = 8
CHUNKS = (4, 2)
SOURCES = 32
LIMIT = 40 << 20
F32, BF16 = jnp.float32, jnp.bfloat16
VMEM = pl.BlockSpec(memory_space=pltpu.VMEM)
HBM = pl.BlockSpec(memory_space=pltpu.HBM)
SWAP = [(0, 1), (1, 0)]
STARTS = [sum(CHUNKS[:c]) for c in range(len(CHUNKS))]


def dot(a, b):
    return jnp.dot(a, b, preferred_element_type=F32)


def iota(shape, dim):
    return lax.broadcasted_iota(jnp.int32, shape, dim)


def where_bf16(condition):
    return jnp.where(condition, 1.0, 0.0).astype(BF16)


def ranks(ids, keep, experts, along):
    tokens = ids[0].shape[along]
    shape = (experts, tokens) if along == 1 else (tokens, experts)
    member = iota(shape, 1 - along)
    hot = [jnp.where((member == ids[k]) & (keep[k] > 0), 1.0, 0.0) for k in (0, 1)]
    older = where_bf16(iota((tokens, tokens), 1 - along) < iota((tokens, tokens), along))
    out = []
    base = 0.0
    for k in (0, 1):
        sent = hot[k].astype(BF16)
        before = (dot(sent, older) if along == 1 else dot(older, sent)) + base
        out.append(jnp.sum(hot[k] * before, axis=1 - along, keepdims=True).astype(jnp.int32))
        base = base + jnp.sum(hot[k], axis=along, keepdims=True)
    return out


def packed_row(ids, keep, rank, chunk, piece):
    slots, slot = CHUNKS[chunk], rank - STARTS[chunk]
    inside = (keep > 0) & (slot >= 0) & (slot < slots)
    return jnp.where(inside, ids * PACK + slots * piece + slot, -1)


def pack_kernel(experts, own_ref, recv_ref, res_ref, gain_ref, ids_ref, keep_ref, stream_ref, *packed_refs):
    stream = (res_ref[...].astype(F32) + (own_ref[...] + recv_ref[...])).astype(BF16)
    stream_ref[...] = stream
    value = stream.astype(F32)
    tokens, features = value.shape
    centred = value - jnp.sum(value, axis=1, keepdims=True) / features
    variance = jnp.sum(centred * centred, axis=1, keepdims=True) / features
    normed = (centred / jnp.sqrt(variance + 1e-05) * gain_ref[...]).astype(BF16)
    ids = [ids_ref[k : k + 1, :] for k in (0, 1)]
    keep = [keep_ref[k : k + 1, :] for k in (0, 1)]
    rank = ranks(ids, keep, experts, 1)
    for chunk, slots in enumerate(CHUNKS):
        pieces = PACK // slots
        wide = features // pieces
        at = [
            jnp.concatenate([packed_row(ids[k], keep[k], rank[k], chunk, h) for h in range(pieces)], axis=1)
            for k in (0, 1)
        ]
        rows = iota((experts * PACK, tokens * pieces), 0)
        stacked = jnp.concatenate([normed[:, h * wide : (h + 1) * wide] for h in range(pieces)], axis=0)
        packed_refs[chunk][...] = dot(where_bf16((rows == at[0]) | (rows == at[1])), stacked).astype(BF16)


def combine_kernel(experts, *refs):
    packed_refs = refs[: len(CHUNKS)]
    stream_ref, ids_ref, keep_ref, gate_ref, out_ref = refs[len(CHUNKS) :]
    ids = [ids_ref[:, k : k + 1] for k in (0, 1)]
    keep = [keep_ref[:, k : k + 1] for k in (0, 1)]
    gate = [gate_ref[:, k : k + 1] for k in (0, 1)]
    rank = ranks(ids, keep, experts, 0)
    tokens, _ = stream_ref.shape
    columns = iota((2 * tokens, experts * PACK), 1)
    total = None
    for chunk, slots in enumerate(CHUNKS):
        pieces = PACK // slots
        packed = packed_refs[chunk][...]
        mixed = []
        for h in range(pieces):
            at = jnp.concatenate([packed_row(ids[k], keep[k], rank[k], chunk, h) for k in (0, 1)], axis=0)
            rows = dot(where_bf16(columns == at), packed)
            mixed.append(gate[0] * rows[:tokens] + gate[1] * rows[tokens:])
        mixed = jnp.concatenate(mixed, axis=1)
        total = mixed if total is None else total + mixed
    out_ref[...] = (stream_ref[...].astype(F32) + total).astype(BF16)


def unpack_matrix(slots, reverse):
    size = SOURCES * PACK
    shift = slots.bit_length() - 1
    row, col = iota((size, size), 1 if reverse else 0), iota((size, size), 0 if reverse else 1)
    source, at = col >> 3, col & 7
    piece, slot = at >> shift, at & (slots - 1)
    return where_bf16(row == piece * (SOURCES * slots) + slots * source + slot)


def ffn_kernel(slots, tile, own_ref, other_ref, in_hbm, out_hbm, own_out, other_out, in_ref, out_ref, rows_ref, hidden_ref, sems):
    _, units = in_hbm.shape
    steps_in, steps_out = units // tile, out_hbm.shape[1] // tile

    def copies(which, i):
        at = pl.ds(pl.multiple_of(i * tile, tile), tile)
        source, target = ((in_hbm, in_ref), (out_hbm, out_ref))[which]
        return pltpu.make_async_copy(source.at[:, at], target.at[:, at], sems.at[which * steps_in + i])

    for i in range(steps_in):
        copies(0, i).start()
    for i in range(steps_out):
        copies(1, i).start()
    tall, short = SOURCES * PACK, SOURCES * slots
    pieces = PACK // slots
    wide = own_ref.shape[1]
    groups = own_ref.shape[0] // tall
    spread = unpack_matrix(slots, False)
    for s, ref in enumerate((own_ref, other_ref)):
        for g in range(groups):
            moved = dot(spread, ref[g * tall : (g + 1) * tall, :]).astype(BF16)
            for h in range(pieces):
                first = (s * groups + g) * short
                rows_ref[first : first + short, h * wide : (h + 1) * wide] = moved[h * short : (h + 1) * short]

    @pl.loop(0, steps_in)
    def _(i):
        copies(0, i).wait()
        at = pl.ds(pl.multiple_of(i * tile, tile), tile)
        hidden_ref[:, at] = jnp.maximum(dot(rows_ref[...], in_ref[:, at]), 0.0).astype(BF16)

    @pl.loop(0, steps_out)
    def _(i):
        copies(1, i).wait()
        at = pl.ds(pl.multiple_of(i * tile, tile), tile)
        rows_ref[:, at] = dot(hidden_ref[...], out_ref[:, at]).astype(BF16)

    gather = unpack_matrix(slots, True)
    for s, ref in enumerate((own_out, other_out)):
        for g in range(groups):
            first = (s * groups + g) * short
            stacked = jnp.concatenate(
                [rows_ref[first : first + short, h * wide : (h + 1) * wide] for h in range(pieces)], axis=0
            )
            ref[g * tall : (g + 1) * tall, :] = dot(gather, stacked).astype(BF16)


def ffn(slots, own, other, weight_in, weight_out, tile=512):
    rows = 2 * own.shape[0] * slots // PACK
    features, units = weight_in.shape
    return pl.pallas_call(
        functools.partial(ffn_kernel, slots, tile),
        in_specs=[VMEM, VMEM, HBM, HBM],
        out_specs=[VMEM, VMEM],
        out_shape=[jax.ShapeDtypeStruct(own.shape, BF16)] * 2,
        scratch_shapes=[
            pltpu.VMEM(weight_in.shape, BF16),
            pltpu.VMEM(weight_out.shape, BF16),
            pltpu.VMEM((rows, features), BF16),
            pltpu.VMEM((rows, units), BF16),
            pltpu.SemaphoreType.DMA((units // tile + features // tile,)),
        ],
        compiler_params=pltpu.CompilerParams(vmem_limit_bytes=LIMIT),
        cost_estimate=pl.CostEstimate(
            flops=4 * rows * features * units, bytes_accessed=4 * features * units, transcendentals=0
        ),
    )(own, other, weight_in, weight_out)


def project_kernel(core_ref, context_ref, weight_ref, own_ref, other_ref):
    both = dot(context_ref[...], weight_ref[...])
    tokens = own_ref.shape[0]
    first = core_ref[0] == 0
    own_ref[...] = jnp.where(first, both[:tokens], both[tokens:])
    other_ref[...] = jnp.where(first, both[tokens:], both[:tokens])


def project(core, context, weight, tile=512):
    tokens, depth = context.shape
    features = weight.shape[1]
    half = jax.ShapeDtypeStruct((tokens // 2, features), F32)
    half_spec = pl.BlockSpec((tokens // 2, tile), lambda f, core: (0, f))
    return pl.pallas_call(
        project_kernel,
        grid_spec=pltpu.PrefetchScalarGridSpec(
            num_scalar_prefetch=1,
            grid=(features // tile,),
            in_specs=[
                pl.BlockSpec((tokens, depth), lambda f, core: (0, 0)),
                pl.BlockSpec((depth, tile), lambda f, core: (0, f)),
            ],
            out_specs=[half_spec, half_spec],
        ),
        out_shape=[half, half],
        compiler_params=pltpu.CompilerParams(vmem_limit_bytes=LIMIT),
        cost_estimate=pl.CostEstimate(
            flops=2 * tokens * depth * features, bytes_accessed=2 * depth * features, transcendentals=0
        ),
        name="project",
    )(core[None], context, weight)


def whole(kernel, out_shape, flops, *args):
    return pl.pallas_call(
        kernel,
        in_specs=[VMEM] * len(args),
        out_specs=jax.tree.map(lambda _: VMEM, out_shape),
        out_shape=out_shape,
        compiler_params=pltpu.CompilerParams(vmem_limit_bytes=16 << 20),
        cost_estimate=pl.CostEstimate(
            flops=flops, bytes_accessed=sum(a.size * a.dtype.itemsize for a in args), transcendentals=0
        ),
    )(*args)


def body(context, out_weight, residual_in, norm_gain, expert_ids, gate_weights, keep_mask, expert_in, expert_out):
    tokens, features = residual_in.shape[1:]
    experts = lax.axis_size("ep")
    own, other = project(
        lax.axis_index("tp"), context[0], pltpu.with_memory_space_constraint(out_weight, pltpu.HBM)
    )
    recv = lax.ppermute(other, "tp", SWAP)
    packed_shapes = [
        jax.ShapeDtypeStruct((experts * PACK, features * slots // PACK), BF16) for slots in CHUNKS
    ]
    flops = sum(2 * tokens * experts * PACK * features for _ in CHUNKS)
    stream, *outgoing = whole(
        functools.partial(pack_kernel, experts),
        [jax.ShapeDtypeStruct((tokens, features), BF16), *packed_shapes],
        flops,
        own, recv, residual_in[0], norm_gain[None, :], expert_ids[0].T, keep_mask[0].T,
    )

    def exchange(packed):
        blocks = packed.reshape(experts, PACK, packed.shape[1])
        return lax.all_to_all(blocks, "ep", split_axis=0, concat_axis=0, tiled=True).reshape(packed.shape)

    weights = [pltpu.with_memory_space_constraint(w[0], pltpu.HBM) for w in (expert_in, expert_out)]
    arrived = []
    for packed in outgoing:
        arrived.append(exchange(packed))
    returned = []
    for slots, rows in zip(CHUNKS, arrived):
        rows_other = lax.ppermute(rows, "tp", SWAP)
        part_own, part_other = ffn(slots, rows, rows_other, *weights)
        part_recv = lax.ppermute(part_other, "tp", SWAP)
        returned.append(exchange((part_own.astype(F32) + part_recv.astype(F32)).astype(BF16)))
    return whole(
        functools.partial(combine_kernel, experts),
        jax.ShapeDtypeStruct((tokens, features), BF16),
        2 * flops,
        *returned, stream, expert_ids[0], keep_mask[0], gate_weights[0],
    )[None]


def solution(mesh):
    return jax.shard_map(
        body,
        mesh=mesh,
        in_specs=(
            P("ep", None, "tp"),
            P("tp", None),
            P("ep", "tp", None),
            P(),
            P("ep", "tp", None),
            P("ep", "tp", None),
            P("ep", "tp", None),
            P("ep", None, "tp"),
            P("ep", "tp", None),
        ),
        out_specs=P("ep", "tp", None),
        check_vma=False,
    )
```

```python
import functools

import jax
import jax.numpy as jnp
from jax import lax
from jax.experimental import pallas as pl
from jax.experimental.pallas import tpu as pltpu
from jax.sharding import PartitionSpec as P


SLOT = 6
PACK = 8
TAIL = 3
SOURCES = 32
TILE = 512
LIMIT = 32 << 20
F32, BF16 = jnp.float32, jnp.bfloat16
VMEM = pl.BlockSpec(memory_space=pltpu.VMEM)
SMEM = pl.BlockSpec(memory_space=pltpu.SMEM)
HBM = pl.BlockSpec(memory_space=pltpu.HBM)
SWAP = [(0, 1), (1, 0)]


def dot(a, b):
    return jnp.dot(a, b, preferred_element_type=F32)


def iota(shape, dim):
    return lax.broadcasted_iota(jnp.int32, shape, dim)


def ones_where(condition):
    return jnp.where(condition, 1.0, 0.0).astype(BF16)


def parts_of(width):
    return [slice(j * (width // TAIL), (j + 1) * (width // TAIL)) for j in range(TAIL)]


def places(ids, keep, experts, along):
    tokens = ids[0].shape[along]
    shape = (experts, tokens) if along == 1 else (tokens, experts)
    member = iota(shape, 1 - along)
    hot = [jnp.where((member == ids[k]) & (keep[k] > 0), 1.0, 0.0) for k in (0, 1)]
    older = ones_where(iota((tokens, tokens), 1 - along) < iota((tokens, tokens), along))
    out = []
    base = 0.0
    for k in (0, 1):
        sent = hot[k].astype(BF16)
        before = (dot(sent, older) if along == 1 else dot(older, sent)) + base
        rank = jnp.sum(hot[k] * before, axis=1 - along, keepdims=True).astype(jnp.int32)
        base = base + jnp.sum(hot[k], axis=along, keepdims=True)
        late = jnp.where(rank >= TAIL, 1, 0)
        kept = keep[k] > 0
        tail = ids[k] * PACK + SLOT + late
        out.append(
            (
                jnp.where(kept, ids[k] * PACK + rank, -1),
                [jnp.where(kept & (rank - TAIL * late == j), tail, -1) for j in range(TAIL)],
            )
        )
    return out


def pack_kernel(experts, own_ref, recv_ref, res_ref, gain_ref, ids_ref, keep_ref, stream_ref, packed_ref):
    attended = own_ref[...] + recv_ref[...].astype(F32)
    stream = (res_ref[...].astype(F32) + attended).astype(BF16)
    stream_ref[...] = stream
    value = stream.astype(F32)
    tokens, features = value.shape
    centred = value - jnp.sum(value, axis=1, keepdims=True) / features
    variance = jnp.sum(centred * centred, axis=1, keepdims=True) / features
    normed = (centred / jnp.sqrt(variance + 1e-05) * gain_ref[...]).astype(BF16)
    ids = [ids_ref[k : k + 1, :] for k in (0, 1)]
    keep = [keep_ref[k : k + 1, :] for k in (0, 1)]
    first, second = places(ids, keep, experts, 1)
    rows = iota((experts * PACK, tokens), 0)
    main = ones_where((rows == first[0]) | (rows == second[0]))
    wide = packed_ref.shape[1]
    for j, part in enumerate(parts_of(wide)):
        tail = ones_where((rows == first[1][j]) | (rows == second[1][j]))
        packed_ref[:, part] = dot(
            jnp.concatenate([main, tail], axis=1), jnp.concatenate([normed[:, part], normed[:, wide:]], axis=0)
        ).astype(BF16)


def combine_kernel(experts, packed_ref, stream_ref, ids_ref, keep_ref, gate_ref, out_ref):
    ids = [ids_ref[:, k : k + 1] for k in (0, 1)]
    keep = [keep_ref[:, k : k + 1] for k in (0, 1)]
    first, second = places(ids, keep, experts, 0)
    tokens = ids[0].shape[0]
    columns = iota((2 * tokens, experts * PACK), 1)
    gate = [gate_ref[:, k : k + 1] for k in (0, 1)]
    wide = packed_ref.shape[1]
    parts = parts_of(wide)

    def finish(at, rows):
        mixed = gate[0] * rows[:tokens] + gate[1] * rows[tokens:]
        out_ref[:, at] = (stream_ref[:, at].astype(F32) + mixed).astype(BF16)

    main = ones_where(columns == jnp.concatenate([first[0], second[0]], axis=0))
    for part in parts:
        finish(part, dot(main, packed_ref[:, part]))
    tails = [ones_where(columns == jnp.concatenate([first[1][j], second[1][j]], axis=0)) for j in range(TAIL)]
    finish(
        slice(wide, None),
        dot(jnp.concatenate(tails, axis=1), jnp.concatenate([packed_ref[:, part] for part in parts], axis=0)),
    )


def movers(reverse):
    tall, short = SOURCES * PACK, SOURCES * SLOT
    shape = (tall, short) if reverse else (short, tall)
    row, col = iota(shape, 1 if reverse else 0), iota(shape, 0 if reverse else 1)
    at = col & (PACK - 1)
    slot = row - SLOT * (col >> 3)
    main = ones_where((at < SLOT) & (slot == at))
    return main, [ones_where((at >= SLOT) & (slot == (at - SLOT) * TAIL + j)) for j in range(TAIL)]


def unpack_into(packed_ref, rows_ref):
    tall, short = SOURCES * PACK, SOURCES * SLOT
    wide = packed_ref.shape[1]
    main, tails = movers(False)
    tails = jnp.concatenate(tails, axis=1)
    for g in range(packed_ref.shape[0] // tall):
        block = packed_ref[g * tall : (g + 1) * tall, :]
        at = slice(g * short, (g + 1) * short)
        rows_ref[at, :wide] = dot(main, block).astype(BF16)
        stacked = jnp.concatenate([block[:, part] for part in parts_of(wide)], axis=0)
        rows_ref[at, wide:] = dot(tails, stacked).astype(BF16)


def tile_copy(hbm_ref, vmem_ref, sems, i):
    at = pl.ds(pl.multiple_of(i * TILE, TILE), TILE)
    return pltpu.make_async_copy(hbm_ref.at[:, at], vmem_ref.at[:, at], sems.at[i])


def start_copies(hbm_ref, vmem_ref, sems):
    for i in range(hbm_ref.shape[1] // TILE):
        tile_copy(hbm_ref, vmem_ref, sems, i).start()


def tiled(hbm_ref, vmem_ref, sems, step):
    @pl.loop(0, hbm_ref.shape[1] // TILE)
    def _(i):
        tile_copy(hbm_ref, vmem_ref, sems, i).wait()
        step(pl.ds(pl.multiple_of(i * TILE, TILE), TILE))


def hidden_kernel(packed_ref, in_hbm, hidden_ref, in_ref, rows_ref, sems):
    start_copies(in_hbm, in_ref, sems)
    unpack_into(packed_ref, rows_ref)

    def step(at):
        hidden_ref[:, at] = jnp.maximum(dot(rows_ref[...], in_ref[:, at]), 0.0).astype(BF16)

    tiled(in_hbm, in_ref, sems, step)


def result_kernel(hidden_ref, out_hbm, result_ref, out_ref, sems):
    start_copies(out_hbm, out_ref, sems)

    def step(at):
        result_ref[:, at] = dot(hidden_ref[...], out_ref[:, at]).astype(result_ref.dtype)

    tiled(out_hbm, out_ref, sems, step)


def both_kernel(packed_ref, in_hbm, out_hbm, result_ref, in_ref, rows_ref, hidden_ref, out_ref, in_sems, out_sems):
    start_copies(in_hbm, in_ref, in_sems)
    start_copies(out_hbm, out_ref, out_sems)
    unpack_into(packed_ref, rows_ref)

    def step_in(at):
        hidden_ref[:, at] = jnp.maximum(dot(rows_ref[...], in_ref[:, at]), 0.0).astype(BF16)

    def step_out(at):
        result_ref[:, at] = dot(hidden_ref[...], out_ref[:, at]).astype(result_ref.dtype)

    tiled(in_hbm, in_ref, in_sems, step_in)
    tiled(out_hbm, out_ref, out_sems, step_out)


def add_kernel(own_ref, recv_ref, packed_ref):
    tall, short = SOURCES * PACK, SOURCES * SLOT
    wide = packed_ref.shape[1]
    main, tails = movers(True)
    for g in range(packed_ref.shape[0] // tall):
        at = slice(g * short, (g + 1) * short)
        block = (own_ref[at, :] + recv_ref[at, :].astype(F32)).astype(BF16)
        for j, part in enumerate(parts_of(wide)):
            packed_ref[g * tall : (g + 1) * tall, part] = dot(
                jnp.concatenate([main, tails[j]], axis=1),
                jnp.concatenate([block[:, part], block[:, wide:]], axis=0),
            ).astype(BF16)


def project_kernel(core_ref, context_hbm, weight_hbm, own_ref, other_ref, context_ref, weight_ref, sem, sems):
    load = pltpu.make_async_copy(context_hbm, context_ref, sem)
    load.start()
    start_copies(weight_hbm, weight_ref, sems)
    load.wait()
    tokens = own_ref.shape[0]
    first = core_ref[0] == 0

    def step(at):
        both = dot(context_ref[...], weight_ref[:, at])
        own_ref[:, at] = jnp.where(first, both[:tokens], both[tokens:])
        other_ref[:, at] = jnp.where(first, both[tokens:], both[:tokens]).astype(BF16)

    tiled(weight_hbm, weight_ref, sems, step)


def call(kernel, flops, out_shape, args, specs=None, scratch=(), limit=LIMIT):
    return pl.pallas_call(
        kernel,
        in_specs=specs or [VMEM] * len(args),
        out_specs=jax.tree.map(lambda _: VMEM, out_shape),
        out_shape=out_shape,
        scratch_shapes=scratch,
        compiler_params=pltpu.CompilerParams(vmem_limit_bytes=limit),
        cost_estimate=pl.CostEstimate(
            flops=flops, bytes_accessed=sum(a.size * a.dtype.itemsize for a in args), transcendentals=0
        ),
    )(*args)


def shape(*dims, dtype=BF16):
    return jax.ShapeDtypeStruct(dims, dtype)


def sems(weight):
    return pltpu.SemaphoreType.DMA((weight.shape[1] // TILE,))


def vmem(a):
    return pltpu.VMEM(a.shape, a.dtype)


def body(context, out_weight, residual_in, norm_gain, expert_ids, gate_weights, keep_mask, expert_in, expert_out):
    tokens, features = residual_in.shape[1:]
    experts = lax.axis_size("ep")
    units = expert_in.shape[2]

    def in_hbm(a):
        return pltpu.with_memory_space_constraint(a, pltpu.HBM)

    context, out_weight = in_hbm(context[0]), in_hbm(out_weight)
    weight_in, weight_out = in_hbm(expert_in[0]), in_hbm(expert_out[0])
    own, other = call(
        project_kernel,
        2 * context.size * features,
        [shape(tokens, features, dtype=F32), shape(tokens, features)],
        (lax.axis_index("tp")[None], context, out_weight),
        specs=[SMEM, HBM, HBM],
        scratch=[vmem(context), vmem(out_weight), pltpu.SemaphoreType.DMA(()), sems(out_weight)],
    )
    recv = lax.ppermute(other, "tp", SWAP)
    packed_shape = shape(experts * PACK, features * SLOT // PACK)
    rows_shape = shape(experts * SLOT, features)
    moving = 4 * tokens * experts * PACK * features
    stream, outgoing = call(
        functools.partial(pack_kernel, experts),
        moving,
        [shape(tokens, features), packed_shape],
        (own, recv, residual_in[0], norm_gain[None, :], expert_ids[0].T, keep_mask[0].T),
    )

    def exchange(packed):
        blocks = packed.reshape(experts, PACK, packed.shape[1])
        return lax.all_to_all(blocks, "ep", split_axis=0, concat_axis=0, tiled=True).reshape(packed.shape)

    rows = exchange(outgoing)
    rows_other = lax.ppermute(rows, "tp", SWAP)
    half = 2 * experts * SLOT * features * units
    row_buffer, hidden_shape = vmem(rows_shape), shape(experts * SLOT, units)
    hidden = call(
        hidden_kernel, half, hidden_shape, (rows, weight_in), specs=[VMEM, HBM],
        scratch=[vmem(weight_in), row_buffer, sems(weight_in)],
    )
    part_other = call(
        both_kernel, 2 * half, rows_shape, (rows_other, weight_in, weight_out), specs=[VMEM, HBM, HBM],
        scratch=[vmem(weight_in), row_buffer, vmem(hidden_shape), vmem(weight_out), sems(weight_in), sems(weight_out)],
    )
    part_recv = lax.ppermute(part_other, "tp", SWAP)
    part_own = call(
        result_kernel, half, shape(*rows_shape.shape, dtype=F32), (hidden, weight_out),
        specs=[VMEM, HBM], scratch=[vmem(weight_out), sems(weight_out)],
    )
    results = call(add_kernel, moving, packed_shape, (part_own, part_recv))
    returned = exchange(results)
    return call(
        functools.partial(combine_kernel, experts),
        2 * moving,
        shape(tokens, features),
        (returned, stream, expert_ids[0], keep_mask[0], gate_weights[0]),
    )[None]


def solution(mesh):
    return jax.shard_map(
        body,
        mesh=mesh,
        in_specs=(
            P("ep", None, "tp"),
            P("tp", None),
            P("ep", "tp", None),
            P(),
            P("ep", "tp", None),
            P("ep", "tp", None),
            P("ep", "tp", None),
            P("ep", None, "tp"),
            P("ep", "tp", None),
        ),
        out_specs=P("ep", "tp", None),
        check_vma=False,
    )
```

```python
import functools

import jax
import jax.numpy as jnp
from jax import lax
from jax.experimental import pallas as pl
from jax.experimental.pallas import tpu as pltpu
from jax.sharding import PartitionSpec as P


SLOT = 6
PACK = 8
TAIL = 3
SOURCES = 32
TILE = 512
PIECE = 256
LIMIT = 16 << 20
F32, BF16 = jnp.float32, jnp.bfloat16
VMEM = pl.BlockSpec(memory_space=pltpu.VMEM)
SMEM = pl.BlockSpec(memory_space=pltpu.SMEM)
HBM = pl.BlockSpec(memory_space=pltpu.HBM)
SWAP = [(0, 1), (1, 0)]


def dot(a, b):
    return jnp.dot(a, b, preferred_element_type=F32)


def iota(shape, dim):
    return lax.broadcasted_iota(jnp.int32, shape, dim)


def ones_where(condition):
    return jnp.where(condition, 1.0, 0.0).astype(BF16)


def parts_of(width):
    return [slice(j * (width // TAIL), (j + 1) * (width // TAIL)) for j in range(TAIL)]


def places(ids, keep, experts, along):
    tokens = ids[0].shape[along]
    shape = (experts, tokens) if along == 1 else (tokens, experts)
    member = iota(shape, 1 - along)
    hot = [jnp.where((member == ids[k]) & (keep[k] > 0), 1.0, 0.0) for k in (0, 1)]
    older = ones_where(iota((tokens, tokens), 1 - along) < iota((tokens, tokens), along))
    out = []
    base = 0.0
    for k in (0, 1):
        sent = hot[k].astype(BF16)
        before = (dot(sent, older) if along == 1 else dot(older, sent)) + base
        rank = jnp.sum(hot[k] * before, axis=1 - along, keepdims=True).astype(jnp.int32)
        base = base + jnp.sum(hot[k], axis=along, keepdims=True)
        late = jnp.where(rank >= TAIL, 1, 0)
        kept = keep[k] > 0
        tail = ids[k] * PACK + SLOT + late
        out.append(
            (
                jnp.where(kept, ids[k] * PACK + rank, -1),
                [jnp.where(kept & (rank - TAIL * late == j), tail, -1) for j in range(TAIL)],
            )
        )
    return out


def select_kernel(experts, ids_ref, keep_ref, ids_t_ref, keep_t_ref, gate_ref, at_ref, choice_ref, gates_ref):
    places_t = places(
        [ids_t_ref[k : k + 1, :] for k in (0, 1)], [keep_t_ref[k : k + 1, :] for k in (0, 1)], experts, 1
    )
    at_ref[...] = jnp.concatenate([row for main, tails in places_t for row in (main, *tails)], axis=0)
    first, second = places(
        [ids_ref[:, k : k + 1] for k in (0, 1)], [keep_ref[:, k : k + 1] for k in (0, 1)], experts, 0
    )
    size = experts * PACK
    columns = iota((choice_ref.shape[0], size), 1)
    for j, (a, b) in enumerate(zip([first[0], *first[1]], [second[0], *second[1]])):
        choice_ref[:, j * size : (j + 1) * size] = ones_where(columns == jnp.concatenate([a, b], axis=0))
    gates_ref[...] = gate_ref[...]


def pack_kernel(own_ref, recv_ref, res_ref, gain_ref, at_ref, stream_ref, packed_ref):
    attended = own_ref[...] + recv_ref[...].astype(F32)
    stream = (res_ref[...].astype(F32) + attended).astype(BF16)
    stream_ref[...] = stream
    value = stream.astype(F32)
    tokens, features = value.shape
    centred = value - jnp.sum(value, axis=1, keepdims=True) / features
    variance = jnp.sum(centred * centred, axis=1, keepdims=True) / features
    normed = (centred / jnp.sqrt(variance + 1e-05) * gain_ref[...]).astype(BF16)
    size, wide = packed_ref.shape
    rows = iota((size, tokens), 0)

    def chosen(j):
        return ones_where((rows == at_ref[j : j + 1, :]) | (rows == at_ref[j + 1 + TAIL : j + 2 + TAIL, :]))

    main = chosen(0)
    for j, part in enumerate(parts_of(wide)):
        packed_ref[:, part] = dot(
            jnp.concatenate([main, chosen(1 + j)], axis=1),
            jnp.concatenate([normed[:, part], normed[:, wide:]], axis=0),
        ).astype(BF16)


def combine_kernel(packed_ref, stream_ref, choice_ref, gate_ref, out_ref):
    size, wide = packed_ref.shape
    tokens = out_ref.shape[0]
    gate = [gate_ref[:, k : k + 1] for k in (0, 1)]
    parts = parts_of(wide)

    def finish(at, rows):
        mixed = gate[0] * rows[:tokens] + gate[1] * rows[tokens:]
        out_ref[:, at] = (stream_ref[:, at].astype(F32) + mixed).astype(BF16)

    for part in parts:
        finish(part, dot(choice_ref[:, :size], packed_ref[:, part]))
    finish(
        slice(wide, None),
        dot(choice_ref[:, size:], jnp.concatenate([packed_ref[:, part] for part in parts], axis=0)),
    )


def movers(reverse):
    tall, short = SOURCES * PACK, SOURCES * SLOT
    shape = (tall, short) if reverse else (short, tall)
    row, col = iota(shape, 1 if reverse else 0), iota(shape, 0 if reverse else 1)
    at = col & (PACK - 1)
    slot = row - SLOT * (col >> 3)
    main = ones_where((at < SLOT) & (slot == at))
    return main, [ones_where((at >= SLOT) & (slot == (at - SLOT) * TAIL + j)) for j in range(TAIL)]


def unpack_into(packed_ref, rows_ref):
    tall, short = SOURCES * PACK, SOURCES * SLOT
    wide = packed_ref.shape[1]
    main, tails = movers(False)
    tails = jnp.concatenate(tails, axis=1)
    for g in range(packed_ref.shape[0] // tall):
        block = packed_ref[g * tall : (g + 1) * tall, :]
        at = slice(g * short, (g + 1) * short)
        rows_ref[at, :wide] = dot(main, block).astype(BF16)
        stacked = jnp.concatenate([block[:, part] for part in parts_of(wide)], axis=0)
        rows_ref[at, wide:] = dot(tails, stacked).astype(BF16)


def tile_copy(hbm_ref, vmem_ref, sems, i):
    at = pl.ds(pl.multiple_of(i * PIECE, PIECE), PIECE)
    return pltpu.make_async_copy(hbm_ref.at[:, at], vmem_ref.at[:, at], sems.at[i])


def start_copies(hbm_ref, vmem_ref, sems):
    for i in range(hbm_ref.shape[1] // PIECE):
        tile_copy(hbm_ref, vmem_ref, sems, i).start()


def tiled(width, step, copies=None):
    def wait(i):
        if copies is not None:
            tile_copy(*copies, i).wait()

    pieces = TILE // PIECE
    first = 0
    if copies is not None:
        first = 1
        for i in range(pieces):
            wait(i)
            step(slice(i * PIECE, (i + 1) * PIECE))

    @pl.loop(first, width // TILE)
    def _(i):
        for p in range(pieces):
            wait(i * pieces + p)
        step(pl.ds(pl.multiple_of(i * TILE, TILE), TILE))


def hidden_kernel(packed_ref, in_hbm, hidden_ref, in_ref, rows_ref, sems):
    start_copies(in_hbm, in_ref, sems)
    unpack_into(packed_ref, rows_ref)

    def step(at):
        hidden_ref[:, at] = jnp.maximum(dot(rows_ref[...], in_ref[:, at]), 0.0).astype(BF16)

    tiled(in_ref.shape[1], step, (in_hbm, in_ref, sems))


def both_kernel(packed_ref, in_ref, out_hbm, result_ref, out_ref, rows_ref, hidden_ref, sems):
    start_copies(out_hbm, out_ref, sems)
    unpack_into(packed_ref, rows_ref)

    def step_in(at):
        hidden_ref[:, at] = jnp.maximum(dot(rows_ref[...], in_ref[:, at]), 0.0).astype(BF16)

    def step_out(at):
        result_ref[:, at] = dot(hidden_ref[...], out_ref[:, at]).astype(result_ref.dtype)

    tiled(in_ref.shape[1], step_in)
    for i in range(out_hbm.shape[1] // PIECE):
        tile_copy(out_hbm, out_ref, sems, i).wait()
    tiled(out_ref.shape[1], step_out)


def result_kernel(hidden_ref, out_ref, result_ref):
    def step(at):
        result_ref[:, at] = dot(hidden_ref[...], out_ref[:, at]).astype(result_ref.dtype)

    tiled(out_ref.shape[1], step)


def add_kernel(own_ref, recv_ref, packed_ref):
    tall, short = SOURCES * PACK, SOURCES * SLOT
    wide = packed_ref.shape[1]
    main, tails = movers(True)
    for g in range(packed_ref.shape[0] // tall):
        at = slice(g * short, (g + 1) * short)
        block = (own_ref[at, :] + recv_ref[at, :].astype(F32)).astype(BF16)
        for j, part in enumerate(parts_of(wide)):
            packed_ref[g * tall : (g + 1) * tall, part] = dot(
                jnp.concatenate([main, tails[j]], axis=1),
                jnp.concatenate([block[:, part], block[:, wide:]], axis=0),
            ).astype(BF16)


def project_kernel(core_ref, context_hbm, weight_hbm, own_ref, other_ref, context_ref, weight_ref, sem, sems):
    load = pltpu.make_async_copy(context_hbm, context_ref, sem)
    load.start()
    start_copies(weight_hbm, weight_ref, sems)
    load.wait()
    tokens = own_ref.shape[0]
    first = core_ref[0] == 0

    def step(at):
        both = dot(context_ref[...], weight_ref[:, at])
        own_ref[:, at] = jnp.where(first, both[:tokens], both[tokens:])
        other_ref[:, at] = jnp.where(first, both[tokens:], both[:tokens]).astype(BF16)

    tiled(weight_ref.shape[1], step, (weight_hbm, weight_ref, sems))


def call(kernel, flops, out_shape, args, specs=None, scratch=(), limit=LIMIT):
    return pl.pallas_call(
        kernel,
        in_specs=specs or [VMEM] * len(args),
        out_specs=jax.tree.map(lambda _: VMEM, out_shape),
        out_shape=out_shape,
        scratch_shapes=scratch,
        compiler_params=pltpu.CompilerParams(vmem_limit_bytes=limit),
        cost_estimate=pl.CostEstimate(
            flops=flops, bytes_accessed=sum(a.size * a.dtype.itemsize for a in args), transcendentals=0
        ),
    )(*args)


def shape(*dims, dtype=BF16):
    return jax.ShapeDtypeStruct(dims, dtype)


def sems(weight):
    return pltpu.SemaphoreType.DMA((weight.shape[1] // PIECE,))


def vmem(a):
    return pltpu.VMEM(a.shape, a.dtype)


def body(context, out_weight, residual_in, norm_gain, expert_ids, gate_weights, keep_mask, expert_in, expert_out):
    tokens, features = residual_in.shape[1:]
    experts = lax.axis_size("ep")
    units = expert_in.shape[2]

    def in_hbm(a):
        return pltpu.with_memory_space_constraint(a, pltpu.HBM)

    context, out_weight = in_hbm(context[0]), in_hbm(out_weight)
    weight_in, weight_out = in_hbm(expert_in[0]), in_hbm(expert_out[0])
    own, other = call(
        project_kernel,
        2 * context.size * features,
        [shape(tokens, features, dtype=F32), shape(tokens, features)],
        (lax.axis_index("tp")[None], context, out_weight),
        specs=[SMEM, HBM, HBM],
        scratch=[vmem(context), vmem(out_weight), pltpu.SemaphoreType.DMA(()), sems(out_weight)],
    )
    recv = lax.ppermute(other, "tp", SWAP)
    ids, keep = expert_ids[0], keep_mask[0]
    at, choice, gates = call(
        functools.partial(select_kernel, experts),
        tokens * tokens * experts * PACK,
        [
            shape(2 + 2 * TAIL, tokens, dtype=jnp.int32),
            shape(2 * tokens, (1 + TAIL) * experts * PACK),
            shape(tokens, 2, dtype=F32),
        ],
        (ids, keep, ids.T, keep.T, gate_weights[0]),
    )
    packed_shape = shape(experts * PACK, features * SLOT // PACK)
    rows_shape = shape(experts * SLOT, features)
    moving = 4 * tokens * experts * PACK * features
    stream, outgoing = call(
        pack_kernel,
        moving,
        [shape(tokens, features), packed_shape],
        (own, recv, residual_in[0], norm_gain[None, :], at),
    )

    def exchange(packed):
        blocks = packed.reshape(experts, PACK, packed.shape[1])
        return lax.all_to_all(blocks, "ep", split_axis=0, concat_axis=0, tiled=True).reshape(packed.shape)

    rows = exchange(outgoing)
    rows_other = lax.ppermute(rows, "tp", SWAP)
    half = 2 * experts * SLOT * features * units
    row_buffer, hidden_shape = vmem(rows_shape), shape(experts * SLOT, units)
    hidden, weight_in = call(
        hidden_kernel, half, [hidden_shape, vmem(weight_in)], (rows, weight_in), specs=[VMEM, HBM],
        scratch=[row_buffer, sems(weight_in)],
    )
    part_other, weight_out = call(
        both_kernel, 2 * half, [rows_shape, vmem(weight_out)], (rows_other, weight_in, weight_out),
        specs=[VMEM, VMEM, HBM], scratch=[row_buffer, vmem(hidden_shape), sems(weight_out)],
    )
    part_recv = lax.ppermute(part_other, "tp", SWAP)
    part_own = call(result_kernel, half, shape(*rows_shape.shape, dtype=F32), (hidden, weight_out))
    results = call(add_kernel, moving, packed_shape, (part_own, part_recv))
    returned = exchange(results)
    return call(combine_kernel, 2 * moving, shape(tokens, features), (returned, stream, choice, gates))[None]


def solution(mesh):
    return jax.shard_map(
        body,
        mesh=mesh,
        in_specs=(
            P("ep", None, "tp"),
            P("tp", None),
            P("ep", "tp", None),
            P(),
            P("ep", "tp", None),
            P("ep", "tp", None),
            P("ep", "tp", None),
            P("ep", None, "tp"),
            P("ep", "tp", None),
        ),
        out_specs=P("ep", "tp", None),
        check_vma=False,
    )
```

```python
import functools

import jax
import jax.numpy as jnp
from jax import lax
from jax.experimental import pallas as pl
from jax.experimental.pallas import tpu as pltpu
from jax.sharding import PartitionSpec as P


SLOT = 6
PACK = 8
SPLIT = (4, 2)
FIRST = (0, 4)
SOURCES = 32
TILE = 512
LIMIT = 16 << 20
F32, BF16 = jnp.float32, jnp.bfloat16
VMEM = pl.BlockSpec(memory_space=pltpu.VMEM)
SMEM = pl.BlockSpec(memory_space=pltpu.SMEM)
HBM = pl.BlockSpec(memory_space=pltpu.HBM)
SWAP = [(0, 1), (1, 0)]


def dot(a, b):
    return jnp.dot(a, b, preferred_element_type=F32)


def iota(shape, dim):
    return lax.broadcasted_iota(jnp.int32, shape, dim)


def ones_where(condition):
    return jnp.where(condition, 1.0, 0.0).astype(BF16)


def kinds(features):
    start = 0
    for kind, slots in enumerate(SPLIT):
        pieces = PACK // slots
        wide = features // pieces
        yield kind, slots, pieces, wide, slice(start, start + wide)
        start += wide


def ranks(ids, keep, experts):
    tokens = ids[0].shape[1]
    member = iota((experts, tokens), 0)
    hot = [jnp.where((member == ids[k]) & (keep[k] > 0), 1.0, 0.0) for k in (0, 1)]
    older = ones_where(iota((tokens, tokens), 0) < iota((tokens, tokens), 1))
    out = []
    base = 0.0
    for k in (0, 1):
        before = dot(hot[k].astype(BF16), older) + base
        out.append(jnp.sum(hot[k] * before, axis=0, keepdims=True).astype(jnp.int32))
        base = base + jnp.sum(hot[k], axis=1, keepdims=True)
    return out


def packed_row(ids, keep, rank, kind, piece):
    slot = rank - FIRST[kind]
    inside = (keep > 0) & (slot >= 0) & (slot < SPLIT[kind])
    return jnp.where(inside, ids * PACK + SPLIT[kind] * piece + slot, -1)


def upright(row):
    size = row.shape[1]
    return jnp.sum(
        jnp.where(iota((size, size), 0) == iota((size, size), 1), row, jnp.zeros((), row.dtype)), axis=1, keepdims=True
    )


def select_kernel(experts, ids_ref, keep_ref, gate_ref, send_ref, take_ref, gates_ref):
    size, tokens = experts * PACK, ids_ref.shape[1]
    ids = [ids_ref[k : k + 1, :] for k in (0, 1)]
    keep = [keep_ref[k : k + 1, :] for k in (0, 1)]
    rank = ranks(ids, keep, experts)
    start = 0
    for kind, slots in enumerate(SPLIT):
        pieces = PACK // slots
        rows = iota((size, pieces * tokens), 0)
        a, b = (
            jnp.concatenate([packed_row(ids[k], keep[k], rank[k], kind, h) for h in range(pieces)], axis=1)
            for k in (0, 1)
        )
        send_ref[:, start : start + pieces * tokens] = ones_where((rows == a) | (rows == b))
        start += pieces * tokens
    ids, keep, rank = ([upright(row) for row in rows] for rows in (ids, keep, rank))
    columns = iota((tokens, size), 1)
    start = 0
    for kind, slots in enumerate(SPLIT):
        for h in range(PACK // slots):
            for k in (0, 1):
                take_ref[start : start + tokens, :] = ones_where(
                    columns == packed_row(ids[k], keep[k], rank[k], kind, h)
                )
                start += tokens
    for k in (0, 1):
        gates_ref[:, k : k + 1] = upright(gate_ref[k : k + 1, :])


def stack_pieces(rows, pieces, wide):
    return jnp.concatenate([rows[:, h * wide : (h + 1) * wide] for h in range(pieces)], axis=0)


def pack_kernel(own_ref, recv_ref, res_ref, gain_ref, send_ref, stream_ref, packed_ref):
    attended = own_ref[...] + recv_ref[...].astype(F32)
    stream = (res_ref[...].astype(F32) + attended).astype(BF16)
    stream_ref[...] = stream
    value = stream.astype(F32)
    tokens, features = value.shape
    centred = value - jnp.sum(value, axis=1, keepdims=True) / features
    variance = jnp.sum(centred * centred, axis=1, keepdims=True) / features
    normed = (centred / jnp.sqrt(variance + 1e-05) * gain_ref[...]).astype(BF16)
    start = 0
    for _, _, pieces, wide, columns in kinds(features):
        send = send_ref[:, start : start + pieces * tokens]
        packed_ref[:, columns] = dot(send, stack_pieces(normed, pieces, wide)).astype(BF16)
        start += pieces * tokens


def combine_kernel(packed_ref, stream_ref, take_ref, gate_ref, out_ref):
    tokens, features = out_ref.shape
    gate = [gate_ref[:, k : k + 1] for k in (0, 1)]
    start = 0
    total = None
    for _, _, pieces, wide, columns in kinds(features):
        count = 2 * pieces * tokens
        rows = dot(take_ref[start : start + count, :], packed_ref[:, columns])
        start += count
        mixed = []
        for h in range(pieces):
            at = 2 * h * tokens
            mixed.append(gate[0] * rows[at : at + tokens] + gate[1] * rows[at + tokens : at + 2 * tokens])
        mixed = jnp.concatenate(mixed, axis=1)
        total = mixed if total is None else total + mixed
    out_ref[...] = (stream_ref[...].astype(F32) + total).astype(BF16)


def mover(slots, reverse):
    size = SOURCES * PACK
    row, col = iota((size, size), 1 if reverse else 0), iota((size, size), 0 if reverse else 1)
    source, at = col >> 3, col & (PACK - 1)
    piece, slot = at >> (slots.bit_length() - 1), at & (slots - 1)
    return ones_where(row == piece * (SOURCES * slots) + slots * source + slot)


def blocks(packed_rows, features):
    tall = SOURCES * PACK
    for g in range(packed_rows // tall):
        start = g * SOURCES * SLOT
        for kind, slots, pieces, wide, columns in kinds(features):
            yield kind, slice(g * tall, (g + 1) * tall), columns, start, SOURCES * slots, pieces, wide
            start += SOURCES * slots


def unpack_into(packed_ref, rows_ref):
    movers = [mover(slots, False) for slots in SPLIT]
    for kind, at, columns, start, count, pieces, wide in blocks(packed_ref.shape[0], rows_ref.shape[1]):
        moved = dot(movers[kind], packed_ref[at, columns]).astype(BF16)
        for h in range(pieces):
            rows_ref[start : start + count, h * wide : (h + 1) * wide] = moved[h * count : (h + 1) * count]


def columns_of(i):
    return pl.ds(pl.multiple_of(i * TILE, TILE), TILE)


def tile_copy(hbm_ref, vmem_ref, sems, i, skip=0):
    return pltpu.make_async_copy(hbm_ref.at[:, columns_of(i + skip)], vmem_ref.at[:, columns_of(i)], sems.at[i])


def start_copies(hbm_ref, vmem_ref, sems, skip=0):
    for i in range(vmem_ref.shape[1] // TILE):
        tile_copy(hbm_ref, vmem_ref, sems, i, skip).start()


def hidden_kernel(packed_ref, first_ref, in_hbm, hidden_ref, rest_ref, rows_ref, sems):
    start_copies(in_hbm, rest_ref, sems, 1)
    unpack_into(packed_ref, rows_ref)
    hidden_ref[:, :TILE] = jnp.maximum(dot(rows_ref[...], first_ref[...]), 0.0).astype(BF16)

    @pl.loop(0, rest_ref.shape[1] // TILE)
    def _(i):
        tile_copy(in_hbm, rest_ref, sems, i, 1).wait()
        hidden_ref[:, columns_of(i + 1)] = jnp.maximum(dot(rows_ref[...], rest_ref[:, columns_of(i)]), 0.0).astype(BF16)


def both_kernel(packed_ref, first_ref, rest_ref, out_hbm, result_ref, out_ref, rows_ref, hidden_ref, sems):
    start_copies(out_hbm, out_ref, sems)
    unpack_into(packed_ref, rows_ref)
    hidden_ref[:, :TILE] = jnp.maximum(dot(rows_ref[...], first_ref[...]), 0.0).astype(BF16)

    @pl.loop(0, rest_ref.shape[1] // TILE)
    def _(i):
        hidden_ref[:, columns_of(i + 1)] = jnp.maximum(dot(rows_ref[...], rest_ref[:, columns_of(i)]), 0.0).astype(BF16)

    @pl.loop(0, out_ref.shape[1] // TILE)
    def _(i):
        tile_copy(out_hbm, out_ref, sems, i).wait()
        result_ref[:, columns_of(i)] = dot(hidden_ref[...], out_ref[:, columns_of(i)]).astype(BF16)


def result_kernel(hidden_ref, out_ref, result_ref):
    @pl.loop(0, out_ref.shape[1] // TILE)
    def _(i):
        result_ref[:, columns_of(i)] = dot(hidden_ref[...], out_ref[:, columns_of(i)])


def add_kernel(own_ref, recv_ref, packed_ref):
    movers = [mover(slots, True) for slots in SPLIT]
    for kind, at, columns, start, count, pieces, wide in blocks(packed_ref.shape[0], own_ref.shape[1]):
        rows = slice(start, start + count)
        block = (own_ref[rows, :] + recv_ref[rows, :].astype(F32)).astype(BF16)
        packed_ref[at, columns] = dot(movers[kind], stack_pieces(block, pieces, wide)).astype(BF16)


def project_kernel(
    core_ref, context_hbm, weight_hbm, in_hbm, own_ref, other_ref, first_ref, context_ref, weight_ref, sem, sems, first_sem
):
    load = pltpu.make_async_copy(context_hbm, context_ref, sem)
    load.start()
    start_copies(weight_hbm, weight_ref, sems)
    start_copies(in_hbm, first_ref, first_sem)
    load.wait()
    tokens = own_ref.shape[0]
    first = core_ref[0] == 0

    @pl.loop(0, weight_ref.shape[1] // TILE)
    def _(i):
        tile_copy(weight_hbm, weight_ref, sems, i).wait()
        at = columns_of(i)
        both = dot(context_ref[...], weight_ref[:, at])
        own_ref[:, at] = jnp.where(first, both[:tokens], both[tokens:])
        other_ref[:, at] = jnp.where(first, both[tokens:], both[:tokens]).astype(BF16)

    tile_copy(in_hbm, first_ref, first_sem, 0).wait()


def call(kernel, flops, out_shape, args, specs=None, scratch=(), limit=LIMIT):
    return pl.pallas_call(
        kernel,
        in_specs=specs or [VMEM] * len(args),
        out_specs=jax.tree.map(lambda _: VMEM, out_shape),
        out_shape=out_shape,
        scratch_shapes=scratch,
        compiler_params=pltpu.CompilerParams(vmem_limit_bytes=limit),
        cost_estimate=pl.CostEstimate(
            flops=flops, bytes_accessed=sum(a.size * a.dtype.itemsize for a in args), transcendentals=0
        ),
    )(*args)


def shape(*dims, dtype=BF16):
    return jax.ShapeDtypeStruct(dims, dtype)


def sems(columns):
    return pltpu.SemaphoreType.DMA((columns // TILE,))


def vmem(a):
    return pltpu.VMEM(a.shape, a.dtype)


def body(context, out_weight, residual_in, norm_gain, expert_ids, gate_weights, keep_mask, expert_in, expert_out):
    tokens, features = residual_in.shape[1:]
    experts = lax.axis_size("ep")
    units = expert_in.shape[2]

    def in_hbm(a):
        return pltpu.with_memory_space_constraint(a, pltpu.HBM)

    context, out_weight = in_hbm(context[0]), in_hbm(out_weight)
    weight_in, weight_out = in_hbm(expert_in[0]), in_hbm(expert_out[0])
    own, other, in_first = call(
        project_kernel,
        2 * context.size * features,
        [shape(tokens, features, dtype=F32), shape(tokens, features), pltpu.VMEM((features, TILE), BF16)],
        (lax.axis_index("tp")[None], context, out_weight, weight_in),
        specs=[SMEM, HBM, HBM, HBM],
        scratch=[vmem(context), vmem(out_weight), pltpu.SemaphoreType.DMA(()), sems(features), sems(TILE)],
    )
    recv = lax.ppermute(other, "tp", SWAP)
    size = experts * PACK
    pieces = sum(PACK // slots for slots in SPLIT)
    send, take, gates = call(
        functools.partial(select_kernel, experts),
        tokens * tokens * size,
        [shape(size, pieces * tokens), shape(2 * pieces * tokens, size), shape(tokens, 2, dtype=F32)],
        (expert_ids[0].T, keep_mask[0].T, gate_weights[0].T),
    )
    packed_shape = shape(experts * PACK, features * SLOT // PACK)
    rows_shape = shape(experts * SLOT, features)
    moving = 4 * tokens * experts * PACK * features
    stream, outgoing = call(
        pack_kernel,
        moving,
        [shape(tokens, features), packed_shape],
        (own, recv, residual_in[0], norm_gain[None, :], send),
    )

    def exchange(packed):
        blocks = packed.reshape(experts, PACK, packed.shape[1])
        return lax.all_to_all(blocks, "ep", split_axis=0, concat_axis=0, tiled=True).reshape(packed.shape)

    rows = exchange(outgoing)
    rows_other = lax.ppermute(rows, "tp", SWAP)
    half = 2 * experts * SLOT * features * units
    row_buffer, hidden_shape = vmem(rows_shape), shape(experts * SLOT, units)
    hidden, in_rest = call(
        hidden_kernel, half, [hidden_shape, pltpu.VMEM((features, units - TILE), BF16)],
        (rows, in_first, weight_in), specs=[VMEM, VMEM, HBM], scratch=[row_buffer, sems(units - TILE)],
    )
    part_other, weight_out = call(
        both_kernel, 2 * half, [rows_shape, vmem(weight_out)],
        (rows_other, in_first, in_rest, weight_out), specs=[VMEM, VMEM, VMEM, HBM],
        scratch=[row_buffer, vmem(hidden_shape), sems(features)],
    )
    part_recv = lax.ppermute(part_other, "tp", SWAP)
    part_own = call(result_kernel, half, shape(*rows_shape.shape, dtype=F32), (hidden, weight_out))
    results = call(add_kernel, moving, packed_shape, (part_own, part_recv))
    returned = exchange(results)
    return call(combine_kernel, 2 * moving, shape(tokens, features), (returned, stream, take, gates))[None]


def solution(mesh):
    return jax.shard_map(
        body,
        mesh=mesh,
        in_specs=(
            P("ep", None, "tp"),
            P("tp", None),
            P("ep", "tp", None),
            P(),
            P("ep", "tp", None),
            P("ep", "tp", None),
            P("ep", "tp", None),
            P("ep", None, "tp"),
            P("ep", "tp", None),
        ),
        out_specs=P("ep", "tp", None),
        check_vma=False,
    )
```

```python
import functools

import jax
import jax.numpy as jnp
from jax import lax
from jax.experimental import pallas as pl
from jax.experimental.pallas import tpu as pltpu
from jax.sharding import PartitionSpec as P


SLOT = 6
PACK = 8
SPLIT = (4, 2)
FIRST = (0, 4)
SOURCES = 32
TILE = 512
LIMIT = 16 << 20
F32, BF16 = jnp.float32, jnp.bfloat16
VMEM = pl.BlockSpec(memory_space=pltpu.VMEM)
SMEM = pl.BlockSpec(memory_space=pltpu.SMEM)
HBM = pl.BlockSpec(memory_space=pltpu.HBM)
SWAP = [(0, 1), (1, 0)]


def dot(a, b):
    return jnp.dot(a, b, preferred_element_type=F32)


def iota(shape, dim):
    return lax.broadcasted_iota(jnp.int32, shape, dim)


def ones_where(condition):
    return jnp.where(condition, 1.0, 0.0).astype(BF16)


def kinds(features):
    start = 0
    for kind, slots in enumerate(SPLIT):
        pieces = PACK // slots
        wide = features // pieces
        yield kind, slots, pieces, wide, slice(start, start + wide)
        start += wide


def ranks(ids, keep, experts):
    tokens = ids[0].shape[1]
    member = iota((experts, tokens), 0)
    hot = [jnp.where((member == ids[k]) & (keep[k] > 0), 1.0, 0.0) for k in (0, 1)]
    older = ones_where(iota((tokens, tokens), 0) < iota((tokens, tokens), 1))
    out = []
    base = 0.0
    for k in (0, 1):
        before = dot(hot[k].astype(BF16), older) + base
        out.append(jnp.sum(hot[k] * before, axis=0, keepdims=True).astype(jnp.int32))
        base = base + jnp.sum(hot[k], axis=1, keepdims=True)
    return out


def packed_row(ids, keep, rank, kind, piece):
    slot = rank - FIRST[kind]
    inside = (keep > 0) & (slot >= 0) & (slot < SPLIT[kind])
    return jnp.where(inside, ids * PACK + SPLIT[kind] * piece + slot, -1)


def upright(row):
    size = row.shape[1]
    return jnp.sum(
        jnp.where(iota((size, size), 0) == iota((size, size), 1), row, jnp.zeros((), row.dtype)), axis=1, keepdims=True
    )


def select_kernel(experts, ids_ref, keep_ref, gate_ref, send_ref, take_ref, gates_ref):
    size, tokens = experts * PACK, ids_ref.shape[1]
    ids = [ids_ref[k : k + 1, :] for k in (0, 1)]
    keep = [keep_ref[k : k + 1, :] for k in (0, 1)]
    rank = ranks(ids, keep, experts)
    start = 0
    for kind, slots in enumerate(SPLIT):
        pieces = PACK // slots
        rows = iota((size, pieces * tokens), 0)
        a, b = (
            jnp.concatenate([packed_row(ids[k], keep[k], rank[k], kind, h) for h in range(pieces)], axis=1)
            for k in (0, 1)
        )
        send_ref[:, start : start + pieces * tokens] = ones_where((rows == a) | (rows == b))
        start += pieces * tokens
    ids, keep, rank = ([upright(row) for row in rows] for rows in (ids, keep, rank))
    columns = iota((tokens, size), 1)
    start = 0
    for kind, slots in enumerate(SPLIT):
        for h in range(PACK // slots):
            for k in (0, 1):
                take_ref[start : start + tokens, :] = ones_where(
                    columns == packed_row(ids[k], keep[k], rank[k], kind, h)
                )
                start += tokens
    for k in (0, 1):
        gates_ref[:, k : k + 1] = upright(gate_ref[k : k + 1, :])


def stack_pieces(rows, pieces, wide):
    return jnp.concatenate([rows[:, h * wide : (h + 1) * wide] for h in range(pieces)], axis=0)


def pack_kernel(own_ref, recv_ref, res_ref, gain_ref, send_ref, stream_ref, packed_ref):
    attended = own_ref[...] + recv_ref[...].astype(F32)
    stream = (res_ref[...].astype(F32) + attended).astype(BF16)
    stream_ref[...] = stream
    value = stream.astype(F32)
    tokens, features = value.shape
    centred = value - jnp.sum(value, axis=1, keepdims=True) / features
    variance = jnp.sum(centred * centred, axis=1, keepdims=True) / features
    normed = (centred / jnp.sqrt(variance + 1e-05) * gain_ref[...]).astype(BF16)
    start = 0
    for _, _, pieces, wide, columns in kinds(features):
        send = send_ref[:, start : start + pieces * tokens]
        packed_ref[:, columns] = dot(send, stack_pieces(normed, pieces, wide)).astype(BF16)
        start += pieces * tokens


def combine_kernel(packed_ref, stream_ref, take_ref, gate_ref, out_hbm, out_ref, sems):
    tokens, features = out_ref.shape
    gate = [gate_ref[:, k : k + 1] for k in (0, 1)]
    start = 0
    taken = []
    for _, _, pieces, wide, columns in kinds(features):
        count = 2 * pieces * tokens
        taken.append((wide, dot(take_ref[start : start + count, :], packed_ref[:, columns])))
        start += count
    part = min(wide for wide, _ in taken)
    copies = []
    for q in range(features // part):
        rows = []
        for k in (0, 1):
            found = []
            for wide, values in taken:
                h, column = q * part // wide, q * part % wide
                found.append(values[(2 * h + k) * tokens : (2 * h + k + 1) * tokens, column : column + part])
            rows.append(sum(found[1:], found[0]))
        at = slice(q * part, (q + 1) * part)
        mixed = gate[0] * rows[0] + gate[1] * rows[1]
        out_ref[:, at] = (stream_ref[:, at].astype(F32) + mixed).astype(BF16)
        copies.append(pltpu.make_async_copy(out_ref.at[:, at], out_hbm.at[:, at], sems.at[q]))
        copies[-1].start()
    for copy in copies:
        copy.wait()


def mover(slots, reverse):
    size = SOURCES * PACK
    row, col = iota((size, size), 1 if reverse else 0), iota((size, size), 0 if reverse else 1)
    source, at = col >> 3, col & (PACK - 1)
    piece, slot = at >> (slots.bit_length() - 1), at & (slots - 1)
    return ones_where(row == piece * (SOURCES * slots) + slots * source + slot)


def blocks(packed_rows, features):
    tall = SOURCES * PACK
    for g in range(packed_rows // tall):
        start = g * SOURCES * SLOT
        for kind, slots, pieces, wide, columns in kinds(features):
            yield kind, slice(g * tall, (g + 1) * tall), columns, start, SOURCES * slots, pieces, wide
            start += SOURCES * slots


def unpack_into(packed_ref, rows_ref):
    movers = [mover(slots, False) for slots in SPLIT]
    for kind, at, columns, start, count, pieces, wide in blocks(packed_ref.shape[0], rows_ref.shape[1]):
        moved = dot(movers[kind], packed_ref[at, columns]).astype(BF16)
        for h in range(pieces):
            rows_ref[start : start + count, h * wide : (h + 1) * wide] = moved[h * count : (h + 1) * count]


def columns_of(i):
    if isinstance(i, int):
        return slice(i * TILE, (i + 1) * TILE)
    return pl.ds(pl.multiple_of(i * TILE, TILE), TILE)


def tile_copy(hbm_ref, vmem_ref, sems, i, skip=0):
    return pltpu.make_async_copy(hbm_ref.at[:, columns_of(i + skip)], vmem_ref.at[:, columns_of(i)], sems.at[i])


def start_copies(hbm_ref, vmem_ref, sems, skip=0):
    for i in range(vmem_ref.shape[1] // TILE):
        tile_copy(hbm_ref, vmem_ref, sems, i, skip).start()


def hidden_kernel(packed_ref, first_ref, in_hbm, hidden_ref, rest_ref, rows_ref, sems):
    start_copies(in_hbm, rest_ref, sems, 1)
    unpack_into(packed_ref, rows_ref)
    hidden_ref[:, :TILE] = jnp.maximum(dot(rows_ref[...], first_ref[...]), 0.0).astype(BF16)
    for i in range(rest_ref.shape[1] // TILE):
        tile_copy(in_hbm, rest_ref, sems, i, 1).wait()
        hidden_ref[:, columns_of(i + 1)] = jnp.maximum(dot(rows_ref[...], rest_ref[:, columns_of(i)]), 0.0).astype(BF16)


def both_kernel(packed_ref, first_ref, rest_ref, out_hbm, result_ref, out_ref, rows_ref, hidden_ref, sems):
    start_copies(out_hbm, out_ref, sems)
    unpack_into(packed_ref, rows_ref)
    hidden_ref[:, :TILE] = jnp.maximum(dot(rows_ref[...], first_ref[...]), 0.0).astype(BF16)
    for i in range(rest_ref.shape[1] // TILE):
        hidden_ref[:, columns_of(i + 1)] = jnp.maximum(dot(rows_ref[...], rest_ref[:, columns_of(i)]), 0.0).astype(BF16)
    for i in range(out_ref.shape[1] // TILE):
        tile_copy(out_hbm, out_ref, sems, i).wait()
    for i in range(out_ref.shape[1] // TILE):
        result_ref[:, columns_of(i)] = dot(hidden_ref[...], out_ref[:, columns_of(i)]).astype(BF16)


def result_kernel(hidden_ref, out_ref, result_ref):
    for i in range(out_ref.shape[1] // TILE):
        result_ref[:, columns_of(i)] = dot(hidden_ref[...], out_ref[:, columns_of(i)])


def add_kernel(own_ref, recv_ref, packed_ref):
    movers = [mover(slots, True) for slots in SPLIT]
    for kind, at, columns, start, count, pieces, wide in blocks(packed_ref.shape[0], own_ref.shape[1]):
        rows = slice(start, start + count)
        block = (own_ref[rows, :] + recv_ref[rows, :].astype(F32)).astype(BF16)
        packed_ref[at, columns] = dot(movers[kind], stack_pieces(block, pieces, wide)).astype(BF16)


def project_kernel(
    core_ref, context_hbm, weight_hbm, in_hbm, own_ref, other_ref, first_ref, context_ref, weight_ref, sem, sems, first_sem
):
    load = pltpu.make_async_copy(context_hbm, context_ref, sem)
    load.start()
    start_copies(weight_hbm, weight_ref, sems)
    start_copies(in_hbm, first_ref, first_sem)
    load.wait()
    tokens = own_ref.shape[0]
    first = core_ref[0] == 0

    @pl.loop(0, weight_ref.shape[1] // TILE)
    def _(i):
        tile_copy(weight_hbm, weight_ref, sems, i).wait()
        at = columns_of(i)
        both = dot(context_ref[...], weight_ref[:, at])
        own_ref[:, at] = jnp.where(first, both[:tokens], both[tokens:])
        other_ref[:, at] = jnp.where(first, both[tokens:], both[:tokens]).astype(BF16)

    tile_copy(in_hbm, first_ref, first_sem, 0).wait()


def call(kernel, flops, out_shape, args, specs=None, out_specs=None, scratch=()):
    return pl.pallas_call(
        kernel,
        in_specs=specs or [VMEM] * len(args),
        out_specs=out_specs or jax.tree.map(lambda _: VMEM, out_shape),
        out_shape=out_shape,
        scratch_shapes=scratch,
        compiler_params=pltpu.CompilerParams(vmem_limit_bytes=LIMIT),
        cost_estimate=pl.CostEstimate(
            flops=flops, bytes_accessed=sum(a.size * a.dtype.itemsize for a in args), transcendentals=0
        ),
    )(*args)


def shape(*dims, dtype=BF16):
    return jax.ShapeDtypeStruct(dims, dtype)


def sems(columns):
    return pltpu.SemaphoreType.DMA((columns // TILE,))


def vmem(a):
    return pltpu.VMEM(a.shape, a.dtype)


def body(context, out_weight, residual_in, norm_gain, expert_ids, gate_weights, keep_mask, expert_in, expert_out):
    tokens, features = residual_in.shape[1:]
    experts = lax.axis_size("ep")
    units = expert_in.shape[2]

    def in_hbm(a):
        return pltpu.with_memory_space_constraint(a, pltpu.HBM)

    context, out_weight = in_hbm(context[0]), in_hbm(out_weight)
    weight_in, weight_out = in_hbm(expert_in[0]), in_hbm(expert_out[0])
    own, other, in_first = call(
        project_kernel,
        2 * context.size * features,
        [shape(tokens, features, dtype=F32), shape(tokens, features), pltpu.VMEM((features, TILE), BF16)],
        (lax.axis_index("tp")[None], context, out_weight, weight_in),
        specs=[SMEM, HBM, HBM, HBM],
        scratch=[vmem(context), vmem(out_weight), pltpu.SemaphoreType.DMA(()), sems(features), sems(TILE)],
    )
    recv = lax.ppermute(other, "tp", SWAP)
    size = experts * PACK
    pieces = sum(PACK // slots for slots in SPLIT)
    send, take, gates = call(
        functools.partial(select_kernel, experts),
        tokens * tokens * size,
        [shape(size, pieces * tokens), shape(2 * pieces * tokens, size), shape(tokens, 2, dtype=F32)],
        (expert_ids[0].T, keep_mask[0].T, gate_weights[0].T),
    )
    packed_shape = shape(experts * PACK, features * SLOT // PACK)
    rows_shape = shape(experts * SLOT, features)
    moving = 4 * tokens * experts * PACK * features
    stream, outgoing = call(
        pack_kernel,
        moving,
        [shape(tokens, features), packed_shape],
        (own, recv, residual_in[0], norm_gain[None, :], send),
    )

    def exchange(packed):
        blocks = packed.reshape(experts, PACK, packed.shape[1])
        return lax.all_to_all(blocks, "ep", split_axis=0, concat_axis=0, tiled=True).reshape(packed.shape)

    rows = exchange(outgoing)
    rows_other = lax.ppermute(rows, "tp", SWAP)
    half = 2 * experts * SLOT * features * units
    row_buffer, hidden_shape = vmem(rows_shape), shape(experts * SLOT, units)
    hidden, in_rest = call(
        hidden_kernel, half, [hidden_shape, pltpu.VMEM((features, units - TILE), BF16)],
        (rows, in_first, weight_in), specs=[VMEM, VMEM, HBM], scratch=[row_buffer, sems(units - TILE)],
    )
    part_other, weight_out = call(
        both_kernel, 2 * half, [rows_shape, vmem(weight_out)],
        (rows_other, in_first, in_rest, weight_out), specs=[VMEM, VMEM, VMEM, HBM],
        scratch=[row_buffer, vmem(hidden_shape), sems(features)],
    )
    part_recv = lax.ppermute(part_other, "tp", SWAP)
    part_own = call(result_kernel, half, shape(*rows_shape.shape, dtype=F32), (hidden, weight_out))
    results = call(add_kernel, moving, packed_shape, (part_own, part_recv))
    returned = exchange(results)
    out_shape = shape(tokens, features)
    return call(
        combine_kernel,
        2 * moving,
        out_shape,
        (returned, stream, take, gates),
        out_specs=HBM,
        scratch=[vmem(out_shape), pltpu.SemaphoreType.DMA((max(PACK // slots for slots in SPLIT),))],
    )[None]


def solution(mesh):
    return jax.shard_map(
        body,
        mesh=mesh,
        in_specs=(
            P("ep", None, "tp"),
            P("tp", None),
            P("ep", "tp", None),
            P(),
            P("ep", "tp", None),
            P("ep", "tp", None),
            P("ep", "tp", None),
            P("ep", None, "tp"),
            P("ep", "tp", None),
        ),
        out_specs=P("ep", "tp", None),
        check_vma=False,
    )
```

```python
import functools

import jax
import jax.numpy as jnp
from jax import lax
from jax.experimental import pallas as pl
from jax.experimental.pallas import tpu as pltpu
from jax.sharding import PartitionSpec as P


SLOT = 6
PACK = 8
SPLIT = (4, 2)
FIRST = (0, 4)
SOURCES = 32
TILE = 512
LIMIT = 16 << 20
F32, BF16 = jnp.float32, jnp.bfloat16
VMEM = pl.BlockSpec(memory_space=pltpu.VMEM)
SMEM = pl.BlockSpec(memory_space=pltpu.SMEM)
HBM = pl.BlockSpec(memory_space=pltpu.HBM)
SWAP = [(0, 1), (1, 0)]


def dot(a, b):
    return jnp.dot(a, b, preferred_element_type=F32)


def iota(shape, dim):
    return lax.broadcasted_iota(jnp.int32, shape, dim)


def ones_where(condition):
    return jnp.where(condition, 1.0, 0.0).astype(BF16)


def kinds(features):
    start = 0
    for kind, slots in enumerate(SPLIT):
        pieces = PACK // slots
        wide = features // pieces
        yield kind, slots, pieces, wide, slice(start, start + wide)
        start += wide


def ranks(ids, keep, experts):
    tokens = ids[0].shape[1]
    member = iota((experts, tokens), 0)
    hot = [jnp.where((member == ids[k]) & (keep[k] > 0), 1.0, 0.0) for k in (0, 1)]
    older = ones_where(iota((tokens, tokens), 0) < iota((tokens, tokens), 1))
    out = []
    base = 0.0
    for k in (0, 1):
        before = dot(hot[k].astype(BF16), older) + base
        out.append(jnp.sum(hot[k] * before, axis=0, keepdims=True).astype(jnp.int32))
        base = base + jnp.sum(hot[k], axis=1, keepdims=True)
    return out


def packed_row(ids, keep, rank, kind, piece):
    slot = rank - FIRST[kind]
    inside = (keep > 0) & (slot >= 0) & (slot < SPLIT[kind])
    return jnp.where(inside, ids * PACK + SPLIT[kind] * piece + slot, -1)


def upright(row):
    size = row.shape[1]
    return jnp.sum(
        jnp.where(iota((size, size), 0) == iota((size, size), 1), row, jnp.zeros((), row.dtype)), axis=1, keepdims=True
    )


def select_kernel(experts, ids_ref, keep_ref, gate_ref, send_ref, take_ref, gates_ref):
    size, tokens = experts * PACK, ids_ref.shape[1]
    ids = [ids_ref[k : k + 1, :] for k in (0, 1)]
    keep = [keep_ref[k : k + 1, :] for k in (0, 1)]
    rank = ranks(ids, keep, experts)
    start = 0
    for kind, slots in enumerate(SPLIT):
        pieces = PACK // slots
        rows = iota((size, pieces * tokens), 0)
        a, b = (
            jnp.concatenate([packed_row(ids[k], keep[k], rank[k], kind, h) for h in range(pieces)], axis=1)
            for k in (0, 1)
        )
        send_ref[:, start : start + pieces * tokens] = ones_where((rows == a) | (rows == b))
        start += pieces * tokens
    ids, keep, rank = ([upright(row) for row in rows] for rows in (ids, keep, rank))
    columns = iota((tokens, size), 1)
    start = 0
    for kind, slots in enumerate(SPLIT):
        for h in range(PACK // slots):
            for k in (0, 1):
                take_ref[start : start + tokens, :] = ones_where(
                    columns == packed_row(ids[k], keep[k], rank[k], kind, h)
                )
                start += tokens
    for k in (0, 1):
        gates_ref[:, k : k + 1] = upright(gate_ref[k : k + 1, :])


def stack_pieces(rows, pieces, wide):
    return jnp.concatenate([rows[:, h * wide : (h + 1) * wide] for h in range(pieces)], axis=0)


def pack_kernel(own_ref, recv_ref, res_ref, gain_ref, send_ref, stream_ref, packed_ref):
    attended = own_ref[...] + recv_ref[...].astype(F32)
    stream = (res_ref[...].astype(F32) + attended).astype(BF16)
    stream_ref[...] = stream
    value = stream.astype(F32)
    tokens, features = value.shape
    centred = value - jnp.sum(value, axis=1, keepdims=True) / features
    variance = jnp.sum(centred * centred, axis=1, keepdims=True) / features
    normed = (centred / jnp.sqrt(variance + 1e-05) * gain_ref[...]).astype(BF16)
    start = 0
    for _, _, pieces, wide, columns in kinds(features):
        send = send_ref[:, start : start + pieces * tokens]
        packed_ref[:, columns] = dot(send, stack_pieces(normed, pieces, wide)).astype(BF16)
        start += pieces * tokens


def combine_kernel(packed_ref, stream_ref, take_ref, gate_ref, out_hbm, out_ref, sems):
    tokens, features = out_ref.shape
    gate = [gate_ref[:, k : k + 1] for k in (0, 1)]
    start = 0
    taken = []
    for _, _, pieces, wide, columns in kinds(features):
        count = 2 * pieces * tokens
        taken.append((wide, dot(take_ref[start : start + count, :], packed_ref[:, columns])))
        start += count
    part = min(wide for wide, _ in taken)
    copies = []
    for q in range(features // part):
        rows = []
        for k in (0, 1):
            found = []
            for wide, values in taken:
                h, column = q * part // wide, q * part % wide
                found.append(values[(2 * h + k) * tokens : (2 * h + k + 1) * tokens, column : column + part])
            rows.append(sum(found[1:], found[0]))
        at = slice(q * part, (q + 1) * part)
        mixed = gate[0] * rows[0] + gate[1] * rows[1]
        out_ref[:, at] = (stream_ref[:, at].astype(F32) + mixed).astype(BF16)
        copies.append(pltpu.make_async_copy(out_ref.at[:, at], out_hbm.at[:, at], sems.at[q]))
        copies[-1].start()
    for copy in copies:
        copy.wait()


def mover(slots, reverse):
    size = SOURCES * PACK
    row, col = iota((size, size), 1 if reverse else 0), iota((size, size), 0 if reverse else 1)
    source, at = col >> 3, col & (PACK - 1)
    piece, slot = at >> (slots.bit_length() - 1), at & (slots - 1)
    return ones_where(row == piece * (SOURCES * slots) + slots * source + slot)


def blocks(packed_rows, features):
    tall = SOURCES * PACK
    for g in range(packed_rows // tall):
        start = g * SOURCES * SLOT
        for kind, slots, pieces, wide, columns in kinds(features):
            yield kind, slice(g * tall, (g + 1) * tall), columns, start, SOURCES * slots, pieces, wide
            start += SOURCES * slots


def unpack_into(packed_ref, rows_ref):
    movers = [mover(slots, False) for slots in SPLIT]
    for kind, at, columns, start, count, pieces, wide in blocks(packed_ref.shape[0], rows_ref.shape[1]):
        moved = dot(movers[kind], packed_ref[at, columns]).astype(BF16)
        for h in range(pieces):
            rows_ref[start : start + count, h * wide : (h + 1) * wide] = moved[h * count : (h + 1) * count]


def columns_of(i):
    return slice(i * TILE, (i + 1) * TILE)


def tile_copy(hbm_ref, vmem_ref, sems, i):
    return pltpu.make_async_copy(hbm_ref.at[:, columns_of(i)], vmem_ref.at[:, columns_of(i)], sems.at[i])


def start_copies(hbm_ref, vmem_ref, sems):
    for i in range(vmem_ref.shape[1] // TILE):
        tile_copy(hbm_ref, vmem_ref, sems, i).start()


def hidden_kernel(packed_ref, in_ref, hidden_ref, rows_ref):
    unpack_into(packed_ref, rows_ref)
    for i in range(in_ref.shape[1] // TILE):
        hidden_ref[:, columns_of(i)] = jnp.maximum(dot(rows_ref[...], in_ref[:, columns_of(i)]), 0.0).astype(BF16)


def both_kernel(packed_ref, in_ref, out_hbm, result_ref, out_ref, rows_ref, hidden_ref, sems):
    start_copies(out_hbm, out_ref, sems)
    hidden_kernel(packed_ref, in_ref, hidden_ref, rows_ref)
    for i in range(out_ref.shape[1] // TILE):
        tile_copy(out_hbm, out_ref, sems, i).wait()
    result_kernel(hidden_ref, out_ref, result_ref)


def result_kernel(hidden_ref, out_ref, result_ref):
    for i in range(out_ref.shape[1] // TILE):
        result_ref[:, columns_of(i)] = dot(hidden_ref[...], out_ref[:, columns_of(i)]).astype(result_ref.dtype)


def add_kernel(own_ref, recv_ref, packed_ref):
    movers = [mover(slots, True) for slots in SPLIT]
    for kind, at, columns, start, count, pieces, wide in blocks(packed_ref.shape[0], own_ref.shape[1]):
        rows = slice(start, start + count)
        block = (own_ref[rows, :] + recv_ref[rows, :].astype(F32)).astype(BF16)
        packed_ref[at, columns] = dot(movers[kind], stack_pieces(block, pieces, wide)).astype(BF16)


def project_kernel(core_ref, context_hbm, weight_hbm, own_ref, other_ref, context_ref, weight_ref, sem, sems):
    load = pltpu.make_async_copy(context_hbm, context_ref, sem)
    load.start()
    start_copies(weight_hbm, weight_ref, sems)
    load.wait()
    tokens = own_ref.shape[0]
    first = core_ref[0] == 0
    for i in range(weight_ref.shape[1] // TILE):
        tile_copy(weight_hbm, weight_ref, sems, i).wait()
        at = columns_of(i)
        both = dot(context_ref[...], weight_ref[:, at])
        own_ref[:, at] = jnp.where(first, both[:tokens], both[tokens:])
        other_ref[:, at] = jnp.where(first, both[tokens:], both[:tokens]).astype(BF16)


def call(kernel, flops, out_shape, args, specs=None, out_specs=None, scratch=(), limit=LIMIT):
    return pl.pallas_call(
        kernel,
        in_specs=specs or [VMEM] * len(args),
        out_specs=out_specs or jax.tree.map(lambda _: VMEM, out_shape),
        out_shape=out_shape,
        scratch_shapes=scratch,
        compiler_params=pltpu.CompilerParams(vmem_limit_bytes=limit),
        cost_estimate=pl.CostEstimate(
            flops=flops, bytes_accessed=sum(a.size * a.dtype.itemsize for a in args), transcendentals=0
        ),
    )(*args)


def shape(*dims, dtype=BF16):
    return jax.ShapeDtypeStruct(dims, dtype)


def sems(columns):
    return pltpu.SemaphoreType.DMA((columns // TILE,))


def vmem(a):
    return pltpu.VMEM(a.shape, a.dtype)


def body(context, out_weight, residual_in, norm_gain, expert_ids, gate_weights, keep_mask, expert_in, expert_out):
    tokens, features = residual_in.shape[1:]
    experts = lax.axis_size("ep")
    units = expert_in.shape[2]

    def in_hbm(a):
        return pltpu.with_memory_space_constraint(a, pltpu.HBM)

    context, out_weight = in_hbm(context[0]), in_hbm(out_weight)
    weight_in, weight_out = expert_in[0], in_hbm(expert_out[0])
    own, other = call(
        project_kernel,
        2 * context.size * features,
        [pltpu.VMEM((tokens, features), F32), pltpu.VMEM((tokens, features), BF16)],
        (lax.axis_index("tp")[None], context, out_weight),
        specs=[SMEM, HBM, HBM],
        scratch=[vmem(context), vmem(out_weight), pltpu.SemaphoreType.DMA(()), sems(features)],
        limit=60 << 20,
    )
    recv = lax.ppermute(other, "tp", SWAP)
    size = experts * PACK
    pieces = sum(PACK // slots for slots in SPLIT)
    send, take, gates = call(
        functools.partial(select_kernel, experts),
        tokens * tokens * size,
        [shape(size, pieces * tokens), shape(2 * pieces * tokens, size), shape(tokens, 2, dtype=F32)],
        (expert_ids[0].T, keep_mask[0].T, gate_weights[0].T),
    )
    packed_shape = shape(experts * PACK, features * SLOT // PACK)
    rows_shape = shape(experts * SLOT, features)
    moving = 4 * tokens * experts * PACK * features
    stream, outgoing = call(
        pack_kernel,
        8 * moving,
        [shape(tokens, features), packed_shape],
        (own, recv, residual_in[0], norm_gain[None, :], send),
    )

    def exchange(packed):
        blocks = packed.reshape(experts, PACK, packed.shape[1])
        return lax.all_to_all(blocks, "ep", split_axis=0, concat_axis=0, tiled=True).reshape(packed.shape)

    rows = exchange(outgoing)
    rows_other = lax.ppermute(rows, "tp", SWAP)
    half = 2 * experts * SLOT * features * units
    row_buffer, hidden_shape = vmem(rows_shape), shape(experts * SLOT, units)
    hidden = call(hidden_kernel, half, hidden_shape, (rows, weight_in), scratch=[row_buffer])
    part_other, weight_out = call(
        both_kernel, 2 * half, [rows_shape, vmem(weight_out)], (rows_other, weight_in, weight_out),
        specs=[VMEM, VMEM, HBM], scratch=[row_buffer, vmem(hidden_shape), sems(features)],
    )
    part_recv = lax.ppermute(part_other, "tp", SWAP)
    part_own = call(result_kernel, half, shape(*rows_shape.shape, dtype=F32), (hidden, weight_out))
    results = call(add_kernel, moving, packed_shape, (part_own, part_recv))
    returned = exchange(results)
    out_shape = shape(tokens, features)
    return call(
        combine_kernel,
        2 * moving,
        out_shape,
        (returned, stream, take, gates),
        out_specs=HBM,
        scratch=[vmem(out_shape), pltpu.SemaphoreType.DMA((max(PACK // slots for slots in SPLIT),))],
    )[None]


def solution(mesh):
    return jax.shard_map(
        body,
        mesh=mesh,
        in_specs=(
            P("ep", None, "tp"),
            P("tp", None),
            P("ep", "tp", None),
            P(),
            P("ep", "tp", None),
            P("ep", "tp", None),
            P("ep", "tp", None),
            P("ep", None, "tp"),
            P("ep", "tp", None),
        ),
        out_specs=P("ep", "tp", None),
        check_vma=False,
    )
```

```python
import functools

import jax
import jax.numpy as jnp
from jax import lax
from jax.experimental import pallas as pl
from jax.experimental.pallas import tpu as pltpu
from jax.sharding import PartitionSpec as P


SLOT = 6
PACK = 8
SPLIT = (4, 2)
FIRST = (0, 4)
SOURCES = 32
TILE = 512
LIMIT = 16 << 20
F32, BF16 = jnp.float32, jnp.bfloat16
VMEM = pl.BlockSpec(memory_space=pltpu.VMEM)
SMEM = pl.BlockSpec(memory_space=pltpu.SMEM)
HBM = pl.BlockSpec(memory_space=pltpu.HBM)
SWAP = [(0, 1), (1, 0)]


def dot(a, b):
    return jnp.dot(a, b, preferred_element_type=F32)


def iota(shape, dim):
    return lax.broadcasted_iota(jnp.int32, shape, dim)


def ones_where(condition):
    return jnp.where(condition, 1.0, 0.0).astype(BF16)


def kinds(features):
    start = 0
    for kind, slots in enumerate(SPLIT):
        pieces = PACK // slots
        wide = features // pieces
        yield kind, slots, pieces, wide, slice(start, start + wide)
        start += wide


def ranks(ids, keep, experts):
    tokens = ids[0].shape[1]
    member = iota((experts, tokens), 0)
    hot = [jnp.where((member == ids[k]) & (keep[k] > 0), 1.0, 0.0) for k in (0, 1)]
    older = ones_where(iota((tokens, tokens), 0) < iota((tokens, tokens), 1))
    out = []
    base = 0.0
    for k in (0, 1):
        before = dot(hot[k].astype(BF16), older) + base
        out.append(jnp.sum(hot[k] * before, axis=0, keepdims=True).astype(jnp.int32))
        base = base + jnp.sum(hot[k], axis=1, keepdims=True)
    return out


def packed_row(ids, keep, rank, kind, piece):
    slot = rank - FIRST[kind]
    inside = (keep > 0) & (slot >= 0) & (slot < SPLIT[kind])
    return jnp.where(inside, ids * PACK + SPLIT[kind] * piece + slot, -1)


def upright(row):
    size = row.shape[1]
    return jnp.sum(
        jnp.where(iota((size, size), 0) == iota((size, size), 1), row, jnp.zeros((), row.dtype)), axis=1, keepdims=True
    )


def select_kernel(experts, ids_ref, keep_ref, gate_ref, send_ref, take_ref, gates_ref):
    size, tokens = experts * PACK, ids_ref.shape[1]
    ids = [ids_ref[k : k + 1, :] for k in (0, 1)]
    keep = [keep_ref[k : k + 1, :] for k in (0, 1)]
    rank = ranks(ids, keep, experts)
    start = 0
    for kind, slots in enumerate(SPLIT):
        pieces = PACK // slots
        rows = iota((size, pieces * tokens), 0)
        a, b = (
            jnp.concatenate([packed_row(ids[k], keep[k], rank[k], kind, h) for h in range(pieces)], axis=1)
            for k in (0, 1)
        )
        send_ref[:, start : start + pieces * tokens] = ones_where((rows == a) | (rows == b))
        start += pieces * tokens
    ids, keep, rank = ([upright(row) for row in rows] for rows in (ids, keep, rank))
    columns = iota((tokens, size), 1)
    start = 0
    for kind, slots in enumerate(SPLIT):
        for h in range(PACK // slots):
            for k in (0, 1):
                take_ref[start : start + tokens, :] = ones_where(
                    columns == packed_row(ids[k], keep[k], rank[k], kind, h)
                )
                start += tokens
    for k in (0, 1):
        gates_ref[:, k : k + 1] = upright(gate_ref[k : k + 1, :])


def stack_pieces(rows, pieces, wide):
    return jnp.concatenate([rows[:, h * wide : (h + 1) * wide] for h in range(pieces)], axis=0)


def pack_kernel(own_ref, recv_ref, res_ref, gain_ref, send_ref, stream_ref, packed_ref):
    attended = own_ref[...] + recv_ref[...].astype(F32)
    stream = (res_ref[...].astype(F32) + attended).astype(BF16)
    stream_ref[...] = stream
    value = stream.astype(F32)
    tokens, features = value.shape
    centred = value - jnp.sum(value, axis=1, keepdims=True) / features
    variance = jnp.sum(centred * centred, axis=1, keepdims=True) / features
    normed = (centred * (1.0 / jnp.sqrt(variance + 1e-05)) * gain_ref[...]).astype(BF16)
    start = 0
    for _, _, pieces, wide, columns in kinds(features):
        send = send_ref[:, start : start + pieces * tokens]
        packed_ref[:, columns] = dot(send, stack_pieces(normed, pieces, wide)).astype(BF16)
        start += pieces * tokens


def combine_kernel(packed_ref, stream_ref, take_ref, gate_ref, out_hbm, out_ref, sems):
    tokens, features = out_ref.shape
    gate = [gate_ref[:, k : k + 1] for k in (0, 1)]
    start = 0
    taken = []
    for _, _, pieces, wide, columns in kinds(features):
        count = 2 * pieces * tokens
        taken.append((wide, dot(take_ref[start : start + count, :], packed_ref[:, columns])))
        start += count
    part = min(wide for wide, _ in taken)
    copies = []
    for q in range(features // part):
        rows = []
        for k in (0, 1):
            found = []
            for wide, values in taken:
                h, column = q * part // wide, q * part % wide
                found.append(values[(2 * h + k) * tokens : (2 * h + k + 1) * tokens, column : column + part])
            rows.append(sum(found[1:], found[0]))
        at = slice(q * part, (q + 1) * part)
        mixed = gate[0] * rows[0] + gate[1] * rows[1]
        out_ref[:, at] = (stream_ref[:, at].astype(F32) + mixed).astype(BF16)
        copies.append(pltpu.make_async_copy(out_ref.at[:, at], out_hbm.at[:, at], sems.at[q]))
        copies[-1].start()
    for copy in copies:
        copy.wait()


def mover(slots, reverse):
    size = SOURCES * PACK
    row, col = iota((size, size), 1 if reverse else 0), iota((size, size), 0 if reverse else 1)
    source, at = col >> 3, col & (PACK - 1)
    piece, slot = at >> (slots.bit_length() - 1), at & (slots - 1)
    return ones_where(row == piece * (SOURCES * slots) + slots * source + slot)


def blocks(packed_rows, features):
    tall = SOURCES * PACK
    for g in range(packed_rows // tall):
        start = g * SOURCES * SLOT
        for kind, slots, pieces, wide, columns in kinds(features):
            yield kind, slice(g * tall, (g + 1) * tall), columns, start, SOURCES * slots, pieces, wide
            start += SOURCES * slots


def unpack_into(packed_ref, rows_ref):
    movers = [mover(slots, False) for slots in SPLIT]
    for kind, at, columns, start, count, pieces, wide in blocks(packed_ref.shape[0], rows_ref.shape[1]):
        moved = dot(movers[kind], packed_ref[at, columns]).astype(BF16)
        for h in range(pieces):
            rows_ref[start : start + count, h * wide : (h + 1) * wide] = moved[h * count : (h + 1) * count]


def columns_of(i):
    return slice(i * TILE, (i + 1) * TILE)


def tile_copy(hbm_ref, vmem_ref, sems, i):
    return pltpu.make_async_copy(hbm_ref.at[:, columns_of(i)], vmem_ref.at[:, columns_of(i)], sems.at[i])


def start_copies(hbm_ref, vmem_ref, sems):
    for i in range(vmem_ref.shape[1] // TILE):
        tile_copy(hbm_ref, vmem_ref, sems, i).start()


def hidden_kernel(packed_ref, in_ref, hidden_ref, rows_ref):
    unpack_into(packed_ref, rows_ref)
    for i in range(in_ref.shape[1] // TILE):
        hidden_ref[:, columns_of(i)] = jnp.maximum(dot(rows_ref[...], in_ref[:, columns_of(i)]), 0.0).astype(BF16)


def both_kernel(packed_ref, in_ref, out_hbm, result_ref, out_ref, rows_ref, hidden_ref, sems):
    start_copies(out_hbm, out_ref, sems)
    hidden_kernel(packed_ref, in_ref, hidden_ref, rows_ref)
    for i in range(out_ref.shape[1] // TILE):
        tile_copy(out_hbm, out_ref, sems, i).wait()
    result_kernel(hidden_ref, out_ref, result_ref)


def result_kernel(hidden_ref, out_ref, result_ref):
    for i in range(out_ref.shape[1] // TILE):
        result_ref[:, columns_of(i)] = dot(hidden_ref[...], out_ref[:, columns_of(i)]).astype(result_ref.dtype)


def add_kernel(own_ref, recv_ref, packed_ref):
    movers = [mover(slots, True) for slots in SPLIT]
    for kind, at, columns, start, count, pieces, wide in blocks(packed_ref.shape[0], own_ref.shape[1]):
        rows = slice(start, start + count)
        block = (own_ref[rows, :] + recv_ref[rows, :].astype(F32)).astype(BF16)
        packed_ref[at, columns] = dot(movers[kind], stack_pieces(block, pieces, wide)).astype(BF16)


def project_tiles(width):
    edges = [*range(0, width, TILE), width - TILE // 2, width]
    return [slice(a, b) for a, b in zip(edges, edges[1:])]


def project_kernel(core_ref, context_hbm, weight_hbm, own_ref, other_ref, context_ref, weight_ref, sem, sems):
    load = pltpu.make_async_copy(context_hbm, context_ref, sem)
    load.start()
    tiles = project_tiles(weight_ref.shape[1])
    copies = [
        pltpu.make_async_copy(weight_hbm.at[:, at], weight_ref.at[:, at], sems.at[i]) for i, at in enumerate(tiles)
    ]
    for copy in copies:
        copy.start()
    load.wait()
    tokens = own_ref.shape[0]
    first = core_ref[0] == 0
    for copy, at in zip(copies, tiles):
        copy.wait()
        both = dot(context_ref[...], weight_ref[:, at])
        own_ref[:, at] = jnp.where(first, both[:tokens], both[tokens:])
        other_ref[:, at] = jnp.where(first, both[tokens:], both[:tokens]).astype(BF16)


def call(kernel, flops, out_shape, args, specs=None, out_specs=None, scratch=(), limit=LIMIT):
    return pl.pallas_call(
        kernel,
        in_specs=specs or [VMEM] * len(args),
        out_specs=out_specs or jax.tree.map(lambda _: VMEM, out_shape),
        out_shape=out_shape,
        scratch_shapes=scratch,
        compiler_params=pltpu.CompilerParams(vmem_limit_bytes=limit),
        cost_estimate=pl.CostEstimate(
            flops=flops, bytes_accessed=sum(a.size * a.dtype.itemsize for a in args), transcendentals=0
        ),
    )(*args)


def shape(*dims, dtype=BF16):
    return jax.ShapeDtypeStruct(dims, dtype)


def sems(columns):
    return pltpu.SemaphoreType.DMA((columns // TILE,))


def vmem(a):
    return pltpu.VMEM(a.shape, a.dtype)


def body(context, out_weight, residual_in, norm_gain, expert_ids, gate_weights, keep_mask, expert_in, expert_out):
    tokens, features = residual_in.shape[1:]
    experts = lax.axis_size("ep")
    units = expert_in.shape[2]

    def in_hbm(a):
        return pltpu.with_memory_space_constraint(a, pltpu.HBM)

    context, out_weight = in_hbm(context[0]), in_hbm(out_weight)
    weight_in, weight_out = expert_in[0], in_hbm(expert_out[0])
    own, other = call(
        project_kernel,
        2 * context.size * features,
        [pltpu.VMEM((tokens, features), F32), pltpu.VMEM((tokens, features), BF16)],
        (lax.axis_index("tp")[None], context, out_weight),
        specs=[SMEM, HBM, HBM],
        scratch=[vmem(context), vmem(out_weight), pltpu.SemaphoreType.DMA(()), sems(features + TILE)],
        limit=60 << 20,
    )
    recv = lax.ppermute(other, "tp", SWAP)
    size = experts * PACK
    pieces = sum(PACK // slots for slots in SPLIT)
    send, take, gates = call(
        functools.partial(select_kernel, experts),
        tokens * tokens * size,
        [shape(size, pieces * tokens), shape(2 * pieces * tokens, size), shape(tokens, 2, dtype=F32)],
        (expert_ids[0].T, keep_mask[0].T, gate_weights[0].T),
    )
    packed_shape = shape(experts * PACK, features * SLOT // PACK)
    rows_shape = shape(experts * SLOT, features)
    moving = 4 * tokens * experts * PACK * features
    stream, outgoing = call(
        pack_kernel,
        8 * moving,
        [shape(tokens, features), packed_shape],
        (own, recv, residual_in[0], norm_gain[None, :], send),
    )

    def exchange(packed):
        blocks = packed.reshape(experts, PACK, packed.shape[1])
        return lax.all_to_all(blocks, "ep", split_axis=0, concat_axis=0, tiled=True).reshape(packed.shape)

    rows = exchange(outgoing)
    rows_other = lax.ppermute(rows, "tp", SWAP)
    half = 2 * experts * SLOT * features * units
    row_buffer, hidden_shape = vmem(rows_shape), shape(experts * SLOT, units)
    hidden = call(hidden_kernel, half, hidden_shape, (rows, weight_in), scratch=[row_buffer])
    part_other, weight_out = call(
        both_kernel, 2 * half, [rows_shape, vmem(weight_out)], (rows_other, weight_in, weight_out),
        specs=[VMEM, VMEM, HBM], scratch=[row_buffer, vmem(hidden_shape), sems(features)],
    )
    part_recv = lax.ppermute(part_other, "tp", SWAP)
    part_own = call(result_kernel, half, shape(*rows_shape.shape, dtype=F32), (hidden, weight_out))
    results = call(add_kernel, moving, packed_shape, (part_own, part_recv))
    returned = exchange(results)
    out_shape = shape(tokens, features)
    return call(
        combine_kernel,
        2 * moving,
        out_shape,
        (returned, stream, take, gates),
        out_specs=HBM,
        scratch=[vmem(out_shape), pltpu.SemaphoreType.DMA((max(PACK // slots for slots in SPLIT),))],
    )[None]


def solution(mesh):
    return jax.shard_map(
        body,
        mesh=mesh,
        in_specs=(
            P("ep", None, "tp"),
            P("tp", None),
            P("ep", "tp", None),
            P(),
            P("ep", "tp", None),
            P("ep", "tp", None),
            P("ep", "tp", None),
            P("ep", None, "tp"),
            P("ep", "tp", None),
        ),
        out_specs=P("ep", "tp", None),
        check_vma=False,
    )
```

```python
import functools

import jax
import jax.numpy as jnp
from jax import lax
from jax.experimental import pallas as pl
from jax.experimental.pallas import tpu as pltpu
from jax.sharding import PartitionSpec as P


SLOT = 6
PACK = 8
SPLIT = (4, 2)
FIRST = (0, 4)
SOURCES = 32
TILE = 512
LIMIT = 16 << 20
F32, BF16 = jnp.float32, jnp.bfloat16
VMEM = pl.BlockSpec(memory_space=pltpu.VMEM)
SMEM = pl.BlockSpec(memory_space=pltpu.SMEM)
HBM = pl.BlockSpec(memory_space=pltpu.HBM)
SWAP = [(0, 1), (1, 0)]


def dot(a, b):
    return jnp.dot(a, b, preferred_element_type=F32)


def iota(shape, dim):
    return lax.broadcasted_iota(jnp.int32, shape, dim)


def ones_where(condition):
    return jnp.where(condition, 1.0, 0.0).astype(BF16)


def kinds(features):
    start = 0
    for kind, slots in enumerate(SPLIT):
        pieces = PACK // slots
        wide = features // pieces
        yield kind, slots, pieces, wide, slice(start, start + wide)
        start += wide


def ranks(ids, keep, experts):
    tokens = ids[0].shape[1]
    member = iota((experts, tokens), 0)
    hot = [jnp.where((member == ids[k]) & (keep[k] > 0), 1.0, 0.0) for k in (0, 1)]
    older = ones_where(iota((tokens, tokens), 0) < iota((tokens, tokens), 1))
    out = []
    base = 0.0
    for k in (0, 1):
        before = dot(hot[k].astype(BF16), older) + base
        out.append(jnp.sum(hot[k] * before, axis=0, keepdims=True).astype(jnp.int32))
        base = base + jnp.sum(hot[k], axis=1, keepdims=True)
    return out


def packed_row(ids, keep, rank, kind, piece):
    slot = rank - FIRST[kind]
    inside = (keep > 0) & (slot >= 0) & (slot < SPLIT[kind])
    return jnp.where(inside, ids * PACK + SPLIT[kind] * piece + slot, -1)


def upright(row):
    size = row.shape[1]
    return jnp.sum(
        jnp.where(iota((size, size), 0) == iota((size, size), 1), row, jnp.zeros((), row.dtype)), axis=1, keepdims=True
    )


def select_kernel(experts, ids_ref, keep_ref, gate_ref, send_ref, take_ref, gates_ref):
    size, tokens = experts * PACK, ids_ref.shape[1]
    ids = [ids_ref[k : k + 1, :] for k in (0, 1)]
    keep = [keep_ref[k : k + 1, :] for k in (0, 1)]
    rank = ranks(ids, keep, experts)
    start = 0
    for kind, slots in enumerate(SPLIT):
        pieces = PACK // slots
        rows = iota((size, pieces * tokens), 0)
        a, b = (
            jnp.concatenate([packed_row(ids[k], keep[k], rank[k], kind, h) for h in range(pieces)], axis=1)
            for k in (0, 1)
        )
        send_ref[:, start : start + pieces * tokens] = ones_where((rows == a) | (rows == b))
        start += pieces * tokens
    ids, keep, rank = ([upright(row) for row in rows] for rows in (ids, keep, rank))
    columns = iota((tokens, size), 1)
    start = 0
    for kind, slots in enumerate(SPLIT):
        for h in range(PACK // slots):
            for k in (0, 1):
                take_ref[start : start + tokens, :] = ones_where(
                    columns == packed_row(ids[k], keep[k], rank[k], kind, h)
                )
                start += tokens
    for k in (0, 1):
        gates_ref[:, k : k + 1] = upright(gate_ref[k : k + 1, :])


def stack_pieces(rows, pieces, wide):
    return jnp.concatenate([rows[:, h * wide : (h + 1) * wide] for h in range(pieces)], axis=0)


def pack_kernel(own_ref, recv_ref, res_ref, gain_ref, send_ref, stream_ref, packed_ref):
    attended = own_ref[...] + recv_ref[...].astype(F32)
    stream = (res_ref[...].astype(F32) + attended).astype(BF16)
    stream_ref[...] = stream
    value = stream.astype(F32)
    tokens, features = value.shape
    centred = value - jnp.sum(value, axis=1, keepdims=True) / features
    variance = jnp.sum(centred * centred, axis=1, keepdims=True) / features
    normed = (centred / jnp.sqrt(variance + 1e-05) * gain_ref[...]).astype(BF16)
    start = 0
    for _, _, pieces, wide, columns in kinds(features):
        send = send_ref[:, start : start + pieces * tokens]
        packed_ref[:, columns] = dot(send, stack_pieces(normed, pieces, wide)).astype(BF16)
        start += pieces * tokens


def combine_kernel(packed_ref, stream_ref, take_ref, gate_ref, out_hbm, out_ref, sems):
    tokens, features = out_ref.shape
    gate = [gate_ref[:, k : k + 1] for k in (0, 1)]
    start = 0
    taken = []
    for _, _, pieces, wide, columns in kinds(features):
        count = 2 * pieces * tokens
        taken.append((wide, dot(take_ref[start : start + count, :], packed_ref[:, columns])))
        start += count
    part = min(wide for wide, _ in taken)
    copies = []
    for q in range(features // part):
        rows = []
        for k in (0, 1):
            found = []
            for wide, values in taken:
                h, column = q * part // wide, q * part % wide
                found.append(values[(2 * h + k) * tokens : (2 * h + k + 1) * tokens, column : column + part])
            rows.append(sum(found[1:], found[0]))
        at = slice(q * part, (q + 1) * part)
        mixed = gate[0] * rows[0] + gate[1] * rows[1]
        out_ref[:, at] = (stream_ref[:, at].astype(F32) + mixed).astype(BF16)
        copies.append(pltpu.make_async_copy(out_ref.at[:, at], out_hbm.at[:, at], sems.at[q]))
        copies[-1].start()
    for copy in copies:
        copy.wait()


def mover(slots, reverse):
    size = SOURCES * PACK
    row, col = iota((size, size), 1 if reverse else 0), iota((size, size), 0 if reverse else 1)
    source, at = col >> 3, col & (PACK - 1)
    piece, slot = at >> (slots.bit_length() - 1), at & (slots - 1)
    return ones_where(row == piece * (SOURCES * slots) + slots * source + slot)


def blocks(packed_rows, features):
    tall = SOURCES * PACK
    for g in range(packed_rows // tall):
        start = g * SOURCES * SLOT
        for kind, slots, pieces, wide, columns in kinds(features):
            yield kind, slice(g * tall, (g + 1) * tall), columns, start, SOURCES * slots, pieces, wide
            start += SOURCES * slots


def unpack_into(packed_ref, rows_ref):
    movers = [mover(slots, False) for slots in SPLIT]
    for kind, at, columns, start, count, pieces, wide in blocks(packed_ref.shape[0], rows_ref.shape[1]):
        moved = dot(movers[kind], packed_ref[at, columns]).astype(BF16)
        for h in range(pieces):
            rows_ref[start : start + count, h * wide : (h + 1) * wide] = moved[h * count : (h + 1) * count]


def columns_of(i):
    return slice(i * TILE, (i + 1) * TILE)


def tile_copy(hbm_ref, vmem_ref, sems, i):
    return pltpu.make_async_copy(hbm_ref.at[:, columns_of(i)], vmem_ref.at[:, columns_of(i)], sems.at[i])


def start_copies(hbm_ref, vmem_ref, sems):
    for i in range(vmem_ref.shape[1] // TILE):
        tile_copy(hbm_ref, vmem_ref, sems, i).start()


def hidden_kernel(packed_ref, in_ref, hidden_ref, rows_ref):
    unpack_into(packed_ref, rows_ref)
    for i in range(in_ref.shape[1] // TILE):
        hidden_ref[:, columns_of(i)] = jnp.maximum(dot(rows_ref[...], in_ref[:, columns_of(i)]), 0.0).astype(BF16)


def both_kernel(packed_ref, in_ref, out_hbm, result_ref, out_ref, rows_ref, hidden_ref, sems):
    start_copies(out_hbm, out_ref, sems)
    hidden_kernel(packed_ref, in_ref, hidden_ref, rows_ref)
    for i in range(out_ref.shape[1] // TILE):
        tile_copy(out_hbm, out_ref, sems, i).wait()
    result_kernel(hidden_ref, out_ref, result_ref)


def result_kernel(hidden_ref, out_ref, result_ref):
    for i in range(out_ref.shape[1] // TILE):
        result_ref[:, columns_of(i)] = dot(hidden_ref[...], out_ref[:, columns_of(i)]).astype(result_ref.dtype)


def add_kernel(own_ref, recv_ref, packed_ref):
    movers = [mover(slots, True) for slots in SPLIT]
    for kind, at, columns, start, count, pieces, wide in blocks(packed_ref.shape[0], own_ref.shape[1]):
        rows = slice(start, start + count)
        block = (own_ref[rows, :] + recv_ref[rows, :].astype(F32)).astype(BF16)
        packed_ref[at, columns] = dot(movers[kind], stack_pieces(block, pieces, wide)).astype(BF16)


def half_of(context_ref, half):
    tokens = context_ref.shape[0] // 2
    return context_ref[pl.ds(pl.multiple_of(half * tokens, tokens), tokens), :]


def project_kernel(experts, core_ref, context_hbm, weight_hbm, *refs):
    small_hbm, refs = refs[:3], refs[3:]
    other_ref, context_ref, weight_ref, *chosen = refs[:6]
    small_refs, (small_sems, sem, sems) = refs[6:9], refs[9:]
    loads = [pltpu.make_async_copy(a, b, small_sems.at[i]) for i, (a, b) in enumerate(zip(small_hbm, small_refs))]
    loads.append(pltpu.make_async_copy(context_hbm, context_ref, sem))
    for load in loads:
        load.start()
    start_copies(weight_hbm, weight_ref, sems)
    for load in loads[:3]:
        load.wait()
    select_kernel(experts, *small_refs, *chosen)
    loads[3].wait()
    rows = half_of(context_ref, 1 - core_ref[0])
    for i in range(weight_ref.shape[1] // TILE):
        tile_copy(weight_hbm, weight_ref, sems, i).wait()
        other_ref[:, columns_of(i)] = dot(rows, weight_ref[:, columns_of(i)]).astype(BF16)


def own_kernel(core_ref, context_ref, weight_ref, own_ref):
    rows = half_of(context_ref, core_ref[0])
    for i in range(weight_ref.shape[1] // TILE):
        own_ref[:, columns_of(i)] = dot(rows, weight_ref[:, columns_of(i)])


def call(kernel, flops, out_shape, args, specs=None, out_specs=None, scratch=(), limit=LIMIT):
    return pl.pallas_call(
        kernel,
        in_specs=specs or [VMEM] * len(args),
        out_specs=out_specs or jax.tree.map(lambda _: VMEM, out_shape),
        out_shape=out_shape,
        scratch_shapes=scratch,
        compiler_params=pltpu.CompilerParams(vmem_limit_bytes=limit),
        cost_estimate=pl.CostEstimate(
            flops=flops, bytes_accessed=sum(a.size * a.dtype.itemsize for a in args), transcendentals=0
        ),
    )(*args)


def shape(*dims, dtype=BF16):
    return jax.ShapeDtypeStruct(dims, dtype)


def sems(columns):
    return pltpu.SemaphoreType.DMA((columns // TILE,))


def vmem(a):
    return pltpu.VMEM(a.shape, a.dtype)


def body(context, out_weight, residual_in, norm_gain, expert_ids, gate_weights, keep_mask, expert_in, expert_out):
    tokens, features = residual_in.shape[1:]
    experts = lax.axis_size("ep")
    units = expert_in.shape[2]

    def in_hbm(a):
        return pltpu.with_memory_space_constraint(a, pltpu.HBM)

    context, out_weight = in_hbm(context[0]), in_hbm(out_weight)
    weight_in, weight_out = expert_in[0], in_hbm(expert_out[0])
    size = experts * PACK
    pieces = sum(PACK // slots for slots in SPLIT)
    core = lax.axis_index("tp")[None]
    small = [in_hbm(a[0].T) for a in (expert_ids, keep_mask, gate_weights)]
    other, context, out_weight, send, take, gates = call(
        functools.partial(project_kernel, experts),
        context.size * features,
        [
            pltpu.VMEM((tokens, features), BF16),
            vmem(context),
            vmem(out_weight),
            pltpu.VMEM((size, pieces * tokens), BF16),
            pltpu.VMEM((2 * pieces * tokens, size), BF16),
            pltpu.VMEM((tokens, 2), F32),
        ],
        (core, context, out_weight, *small),
        specs=[SMEM] + [HBM] * 5,
        scratch=[*map(vmem, small), pltpu.SemaphoreType.DMA((3,)), pltpu.SemaphoreType.DMA(()), sems(features)],
        limit=54 << 20,
    )
    recv = lax.ppermute(other, "tp", SWAP)
    own = call(
        own_kernel, context.size * features, shape(tokens, features, dtype=F32), (core, context, out_weight),
        specs=[SMEM, VMEM, VMEM],
    )
    packed_shape = shape(experts * PACK, features * SLOT // PACK)
    rows_shape = shape(experts * SLOT, features)
    moving = 4 * tokens * experts * PACK * features
    stream, outgoing = call(
        pack_kernel,
        8 * moving,
        [shape(tokens, features), packed_shape],
        (own, recv, residual_in[0], norm_gain[None, :], send),
    )

    def exchange(packed):
        blocks = packed.reshape(experts, PACK, packed.shape[1])
        return lax.all_to_all(blocks, "ep", split_axis=0, concat_axis=0, tiled=True).reshape(packed.shape)

    rows = exchange(outgoing)
    rows_other = lax.ppermute(rows, "tp", SWAP)
    half = 2 * experts * SLOT * features * units
    row_buffer, hidden_shape = vmem(rows_shape), shape(experts * SLOT, units)
    hidden = call(hidden_kernel, half, hidden_shape, (rows, weight_in), scratch=[row_buffer])
    part_other, weight_out = call(
        both_kernel, 2 * half, [rows_shape, vmem(weight_out)], (rows_other, weight_in, weight_out),
        specs=[VMEM, VMEM, HBM], scratch=[row_buffer, vmem(hidden_shape), sems(features)],
    )
    part_recv = lax.ppermute(part_other, "tp", SWAP)
    part_own = call(result_kernel, half, shape(*rows_shape.shape, dtype=F32), (hidden, weight_out))
    results = call(add_kernel, moving, packed_shape, (part_own, part_recv))
    returned = exchange(results)
    out_shape = shape(tokens, features)
    return call(
        combine_kernel,
        2 * moving,
        out_shape,
        (returned, stream, take, gates),
        out_specs=HBM,
        scratch=[vmem(out_shape), pltpu.SemaphoreType.DMA((max(PACK // slots for slots in SPLIT),))],
    )[None]


def solution(mesh):
    return jax.shard_map(
        body,
        mesh=mesh,
        in_specs=(
            P("ep", None, "tp"),
            P("tp", None),
            P("ep", "tp", None),
            P(),
            P("ep", "tp", None),
            P("ep", "tp", None),
            P("ep", "tp", None),
            P("ep", None, "tp"),
            P("ep", "tp", None),
        ),
        out_specs=P("ep", "tp", None),
        check_vma=False,
    )
```

```python
import functools

import jax
import jax.numpy as jnp
from jax import lax
from jax.experimental import pallas as pl
from jax.experimental.pallas import tpu as pltpu
from jax.sharding import PartitionSpec as P


SLOT = 6
PACK = 8
SPLIT = (4, 2)
FIRST = (0, 4)
SOURCES = 32
TILE = 512
DEPTH = 512
LIMIT = 16 << 20
F32, BF16 = jnp.float32, jnp.bfloat16
VMEM = pl.BlockSpec(memory_space=pltpu.VMEM)
SMEM = pl.BlockSpec(memory_space=pltpu.SMEM)
HBM = pl.BlockSpec(memory_space=pltpu.HBM)
SWAP = [(0, 1), (1, 0)]


def dot(a, b):
    return jnp.dot(a, b, preferred_element_type=F32)


def iota(shape, dim):
    return lax.broadcasted_iota(jnp.int32, shape, dim)


def ones_where(condition):
    return jnp.where(condition, 1.0, 0.0).astype(BF16)


def kinds(features):
    start = 0
    for kind, slots in enumerate(SPLIT):
        pieces = PACK // slots
        wide = features // pieces
        yield kind, slots, pieces, wide, slice(start, start + wide)
        start += wide


def ranks(ids, keep, experts):
    tokens = ids[0].shape[1]
    member = iota((experts, tokens), 0)
    hot = [jnp.where((member == ids[k]) & (keep[k] > 0), 1.0, 0.0) for k in (0, 1)]
    older = ones_where(iota((tokens, tokens), 0) < iota((tokens, tokens), 1))
    out = []
    base = 0.0
    for k in (0, 1):
        before = dot(hot[k].astype(BF16), older) + base
        out.append(jnp.sum(hot[k] * before, axis=0, keepdims=True).astype(jnp.int32))
        base = base + jnp.sum(hot[k], axis=1, keepdims=True)
    return out


def packed_row(ids, keep, rank, kind, piece):
    slot = rank - FIRST[kind]
    inside = (keep > 0) & (slot >= 0) & (slot < SPLIT[kind])
    return jnp.where(inside, ids * PACK + SPLIT[kind] * piece + slot, -1)


def upright(row):
    size = row.shape[1]
    return jnp.sum(
        jnp.where(iota((size, size), 0) == iota((size, size), 1), row, jnp.zeros((), row.dtype)), axis=1, keepdims=True
    )


def select_kernel(experts, ids_ref, keep_ref, gate_ref, send_ref, take_ref, gates_ref):
    size, tokens = experts * PACK, ids_ref.shape[1]
    ids = [ids_ref[k : k + 1, :] for k in (0, 1)]
    keep = [keep_ref[k : k + 1, :] for k in (0, 1)]
    rank = ranks(ids, keep, experts)
    start = 0
    for kind, slots in enumerate(SPLIT):
        pieces = PACK // slots
        rows = iota((size, pieces * tokens), 0)
        a, b = (
            jnp.concatenate([packed_row(ids[k], keep[k], rank[k], kind, h) for h in range(pieces)], axis=1)
            for k in (0, 1)
        )
        send_ref[:, start : start + pieces * tokens] = ones_where((rows == a) | (rows == b))
        start += pieces * tokens
    ids, keep, rank = ([upright(row) for row in rows] for rows in (ids, keep, rank))
    columns = iota((tokens, size), 1)
    start = 0
    for kind, slots in enumerate(SPLIT):
        for h in range(PACK // slots):
            for k in (0, 1):
                take_ref[start : start + tokens, :] = ones_where(
                    columns == packed_row(ids[k], keep[k], rank[k], kind, h)
                )
                start += tokens
    for k in (0, 1):
        gates_ref[:, k : k + 1] = upright(gate_ref[k : k + 1, :])


def stack_pieces(rows, pieces, wide):
    return jnp.concatenate([rows[:, h * wide : (h + 1) * wide] for h in range(pieces)], axis=0)


def pack_kernel(own_ref, recv_ref, res_ref, gain_ref, send_ref, stream_ref, packed_ref):
    attended = own_ref[...] + recv_ref[...].astype(F32)
    stream = (res_ref[...].astype(F32) + attended).astype(BF16)
    stream_ref[...] = stream
    value = stream.astype(F32)
    tokens, features = value.shape
    centred = value - jnp.sum(value, axis=1, keepdims=True) / features
    variance = jnp.sum(centred * centred, axis=1, keepdims=True) / features
    normed = (centred / jnp.sqrt(variance + 1e-05) * gain_ref[...]).astype(BF16)
    start = 0
    for _, _, pieces, wide, columns in kinds(features):
        send = send_ref[:, start : start + pieces * tokens]
        packed_ref[:, columns] = dot(send, stack_pieces(normed, pieces, wide)).astype(BF16)
        start += pieces * tokens


def combine_kernel(packed_ref, stream_ref, take_ref, gate_ref, out_hbm, out_ref, sems):
    tokens, features = out_ref.shape
    gate = [gate_ref[:, k : k + 1] for k in (0, 1)]
    start = 0
    taken = []
    for _, _, pieces, wide, columns in kinds(features):
        count = 2 * pieces * tokens
        taken.append((wide, dot(take_ref[start : start + count, :], packed_ref[:, columns])))
        start += count
    part = min(wide for wide, _ in taken)
    copies = []
    for q in range(features // part):
        rows = []
        for k in (0, 1):
            found = []
            for wide, values in taken:
                h, column = q * part // wide, q * part % wide
                found.append(values[(2 * h + k) * tokens : (2 * h + k + 1) * tokens, column : column + part])
            rows.append(sum(found[1:], found[0]))
        at = slice(q * part, (q + 1) * part)
        mixed = gate[0] * rows[0] + gate[1] * rows[1]
        out_ref[:, at] = (stream_ref[:, at].astype(F32) + mixed).astype(BF16)
        copies.append(pltpu.make_async_copy(out_ref.at[:, at], out_hbm.at[:, at], sems.at[q]))
        copies[-1].start()
    for copy in copies:
        copy.wait()


def mover(slots, reverse):
    size = SOURCES * PACK
    row, col = iota((size, size), 1 if reverse else 0), iota((size, size), 0 if reverse else 1)
    source, at = col >> 3, col & (PACK - 1)
    piece, slot = at >> (slots.bit_length() - 1), at & (slots - 1)
    return ones_where(row == piece * (SOURCES * slots) + slots * source + slot)


def blocks(packed_rows, features):
    tall = SOURCES * PACK
    for g in range(packed_rows // tall):
        start = g * SOURCES * SLOT
        for kind, slots, pieces, wide, columns in kinds(features):
            yield kind, slice(g * tall, (g + 1) * tall), columns, start, SOURCES * slots, pieces, wide
            start += SOURCES * slots


def unpack_into(packed_ref, rows_ref):
    movers = [mover(slots, False) for slots in SPLIT]
    for kind, at, columns, start, count, pieces, wide in blocks(packed_ref.shape[0], rows_ref.shape[1]):
        moved = dot(movers[kind], packed_ref[at, columns]).astype(BF16)
        for h in range(pieces):
            rows_ref[start : start + count, h * wide : (h + 1) * wide] = moved[h * count : (h + 1) * count]


def columns_of(i):
    return slice(i * TILE, (i + 1) * TILE)


def tile_copy(hbm_ref, vmem_ref, sems, i):
    return pltpu.make_async_copy(hbm_ref.at[:, columns_of(i)], vmem_ref.at[:, columns_of(i)], sems.at[i])


def start_copies(hbm_ref, vmem_ref, sems):
    for i in range(vmem_ref.shape[1] // TILE):
        tile_copy(hbm_ref, vmem_ref, sems, i).start()


def hidden_kernel(packed_ref, in_ref, hidden_ref, rows_ref):
    unpack_into(packed_ref, rows_ref)
    for i in range(in_ref.shape[1] // TILE):
        hidden_ref[:, columns_of(i)] = jnp.maximum(dot(rows_ref[...], in_ref[:, columns_of(i)]), 0.0).astype(BF16)


def both_kernel(packed_ref, in_ref, out_hbm, result_ref, out_ref, rows_ref, hidden_ref, sems):
    start_copies(out_hbm, out_ref, sems)
    hidden_kernel(packed_ref, in_ref, hidden_ref, rows_ref)
    for i in range(out_ref.shape[1] // TILE):
        tile_copy(out_hbm, out_ref, sems, i).wait()
    result_kernel(hidden_ref, out_ref, result_ref)


def result_kernel(hidden_ref, out_ref, result_ref):
    for i in range(out_ref.shape[1] // TILE):
        result_ref[:, columns_of(i)] = dot(hidden_ref[...], out_ref[:, columns_of(i)]).astype(result_ref.dtype)


def add_kernel(own_ref, recv_ref, packed_ref):
    movers = [mover(slots, True) for slots in SPLIT]
    for kind, at, columns, start, count, pieces, wide in blocks(packed_ref.shape[0], own_ref.shape[1]):
        rows = slice(start, start + count)
        block = (own_ref[rows, :] + recv_ref[rows, :].astype(F32)).astype(BF16)
        packed_ref[at, columns] = dot(movers[kind], stack_pieces(block, pieces, wide)).astype(BF16)


def half_of(context_ref, half, columns=slice(None)):
    tokens = context_ref.shape[0] // 2
    return context_ref[pl.ds(pl.multiple_of(half * tokens, tokens), tokens), columns]


def project_kernel(experts, core_ref, context_hbm, weight_hbm, *refs):
    small_hbm, refs = refs[:3], refs[3:]
    other_ref, context_ref, weight_ref, *chosen = refs[:6]
    small_refs, (total_ref, small_sems, sem, sems) = refs[6:9], refs[9:]
    loads = [pltpu.make_async_copy(a, b, small_sems.at[i]) for i, (a, b) in enumerate(zip(small_hbm, small_refs))]
    loads.append(pltpu.make_async_copy(context_hbm, context_ref, sem))
    for load in loads:
        load.start()
    parts = [slice(i * DEPTH, (i + 1) * DEPTH) for i in range(weight_ref.shape[0] // DEPTH)]
    copies = [pltpu.make_async_copy(weight_hbm.at[at, :], weight_ref.at[at, :], sems.at[i]) for i, at in enumerate(parts)]
    for copy in copies:
        copy.start()
    for load in loads[:3]:
        load.wait()
    select_kernel(experts, *small_refs, *chosen)
    loads[3].wait()
    for i, (copy, at) in enumerate(zip(copies, parts)):
        copy.wait()
        term = dot(half_of(context_ref, 1 - core_ref[0], at), weight_ref[at, :])
        if i == 0:
            total_ref[...] = term
        elif i < len(parts) - 1:
            total_ref[...] += term
        else:
            other_ref[...] = (total_ref[...] + term).astype(BF16)


def own_kernel(core_ref, context_ref, weight_ref, own_ref):
    rows = half_of(context_ref, core_ref[0])
    for i in range(weight_ref.shape[1] // TILE):
        own_ref[:, columns_of(i)] = dot(rows, weight_ref[:, columns_of(i)])


def call(kernel, flops, out_shape, args, specs=None, out_specs=None, scratch=(), limit=LIMIT):
    return pl.pallas_call(
        kernel,
        in_specs=specs or [VMEM] * len(args),
        out_specs=out_specs or jax.tree.map(lambda _: VMEM, out_shape),
        out_shape=out_shape,
        scratch_shapes=scratch,
        compiler_params=pltpu.CompilerParams(vmem_limit_bytes=limit),
        cost_estimate=pl.CostEstimate(
            flops=flops, bytes_accessed=sum(a.size * a.dtype.itemsize for a in args), transcendentals=0
        ),
    )(*args)


def shape(*dims, dtype=BF16):
    return jax.ShapeDtypeStruct(dims, dtype)


def sems(columns):
    return pltpu.SemaphoreType.DMA((columns // TILE,))


def vmem(a):
    return pltpu.VMEM(a.shape, a.dtype)


def body(context, out_weight, residual_in, norm_gain, expert_ids, gate_weights, keep_mask, expert_in, expert_out):
    tokens, features = residual_in.shape[1:]
    experts = lax.axis_size("ep")
    units = expert_in.shape[2]

    def in_hbm(a):
        return pltpu.with_memory_space_constraint(a, pltpu.HBM)

    context, out_weight = in_hbm(context[0]), in_hbm(out_weight)
    weight_in, weight_out = expert_in[0], in_hbm(expert_out[0])
    size = experts * PACK
    pieces = sum(PACK // slots for slots in SPLIT)
    core = lax.axis_index("tp")[None]
    small = [in_hbm(a[0].T) for a in (expert_ids, keep_mask, gate_weights)]
    other, context, out_weight, send, take, gates = call(
        functools.partial(project_kernel, experts),
        context.size * features,
        [
            pltpu.VMEM((tokens, features), BF16),
            vmem(context),
            vmem(out_weight),
            pltpu.VMEM((size, pieces * tokens), BF16),
            pltpu.VMEM((2 * pieces * tokens, size), BF16),
            pltpu.VMEM((tokens, 2), F32),
        ],
        (core, context, out_weight, *small),
        specs=[SMEM] + [HBM] * 5,
        scratch=[
            *map(vmem, small),
            pltpu.VMEM((tokens, features), F32),
            pltpu.SemaphoreType.DMA((3,)),
            pltpu.SemaphoreType.DMA(()),
            pltpu.SemaphoreType.DMA((out_weight.shape[0] // DEPTH,)),
        ],
        limit=54 << 20,
    )
    recv = lax.ppermute(other, "tp", SWAP)
    own = call(
        own_kernel, context.size * features, shape(tokens, features, dtype=F32), (core, context, out_weight),
        specs=[SMEM, VMEM, VMEM],
    )
    packed_shape = shape(experts * PACK, features * SLOT // PACK)
    rows_shape = shape(experts * SLOT, features)
    moving = 4 * tokens * experts * PACK * features
    stream, outgoing = call(
        pack_kernel,
        8 * moving,
        [shape(tokens, features), packed_shape],
        (own, recv, residual_in[0], norm_gain[None, :], send),
    )

    def exchange(packed):
        blocks = packed.reshape(experts, PACK, packed.shape[1])
        return lax.all_to_all(blocks, "ep", split_axis=0, concat_axis=0, tiled=True).reshape(packed.shape)

    rows = exchange(outgoing)
    rows_other = lax.ppermute(rows, "tp", SWAP)
    half = 2 * experts * SLOT * features * units
    row_buffer, hidden_shape = vmem(rows_shape), shape(experts * SLOT, units)
    hidden = call(hidden_kernel, half, hidden_shape, (rows, weight_in), scratch=[row_buffer])
    part_other, weight_out = call(
        both_kernel, 2 * half, [rows_shape, vmem(weight_out)], (rows_other, weight_in, weight_out),
        specs=[VMEM, VMEM, HBM], scratch=[row_buffer, vmem(hidden_shape), sems(features)],
    )
    part_recv = lax.ppermute(part_other, "tp", SWAP)
    part_own = call(result_kernel, half, shape(*rows_shape.shape, dtype=F32), (hidden, weight_out))
    results = call(add_kernel, moving, packed_shape, (part_own, part_recv))
    returned = exchange(results)
    out_shape = shape(tokens, features)
    return call(
        combine_kernel,
        2 * moving,
        out_shape,
        (returned, stream, take, gates),
        out_specs=HBM,
        scratch=[vmem(out_shape), pltpu.SemaphoreType.DMA((max(PACK // slots for slots in SPLIT),))],
    )[None]


def solution(mesh):
    return jax.shard_map(
        body,
        mesh=mesh,
        in_specs=(
            P("ep", None, "tp"),
            P("tp", None),
            P("ep", "tp", None),
            P(),
            P("ep", "tp", None),
            P("ep", "tp", None),
            P("ep", "tp", None),
            P("ep", None, "tp"),
            P("ep", "tp", None),
        ),
        out_specs=P("ep", "tp", None),
        check_vma=False,
    )
```
